128 devices in a mesh: ex: 16 (over x, z), ey: 8 (over y, core).
Axes of the slice: x: 4, y: 4, z: 4, core: 2. Of those that a mesh axis runs over, the one named last changes fastest.
Arguments:
- crm_state: float32 [5, 12, 32, 16384], P(None, None, None, ('ex', 'ey')), may hold values from -6 to 6
- gcm_state: float32 [5, 12, 64, 16, 4, 4], P(None, None, 'ex', 'ey'), may hold values from -6 to 6
- mass: float32 [12, 64, 16, 4, 4], P(None, 'ex', 'ey'), may hold values from 0.5 to 2
- dest: int32 [16384, 1], P(('ex', 'ey')), may hold values from 0 to 127; in each aligned block of 128 rows (0 to 127, 128 to 255, ...) at most 2 rows name the same one
- cost_class: int32 [16384], P(('ex', 'ey')), may hold values from 1 to 2
Outputs:
- cloud_slots: float32 [5, 12, 32, 32768], P(None, None, None, ('ex', 'ey'))
- gcm_out: float32 [5, 12, 64, 16, 4, 4], P(None, None, 'ex', 'ey')
The draws below stay inside these ranges and needn't reach their ends.
Inputs may be any that keep to these rules, and one draw needn't show every extreme that they name: Among the 128 columns of one device's block, at most 2 have the same dest, and some block reaches 2.
All inputs are finite; a program needn't handle non-finite values.
Results may differ from the reference program's by a relative error of at most 0.00002.
Values sent between devices are 32-bit elements; how exact they have to be, the bound alone decides.
A program may use at most 128 MiB of HBM per device.

```python
import math
import jax
import jax.numpy as jnp
import numpy as np

F = 5
NZ = 12
NX = 32
NP = 4
ELX = 4
ELY = 2
EXT = 64
EYT = 16
COL_DEV = 128
COLUMNS = 16384
CAP = 2
SLOTS = 256
N_EX = 16
N_EY = 8
DEVICES = 128


def with_ends(array, key, low, largest):
    index_at = [jax.random.randint(jax.random.fold_in(key, axis), (), 0, length) for axis, length in enumerate(array.shape)]
    main_axis = array.shape.index(max(array.shape))
    beside = index_at[:main_axis] + [(index_at[main_axis] + 1) % array.shape[main_axis]] + index_at[main_axis + 1:]
    return array.at[tuple(index_at)].set(low).at[tuple(beside)].set(largest)


def steps_of(own_key, shape, pieces, low, top_value):
    def one(axis_at, shards_of):
        steps = jax.random.uniform(jax.random.fold_in(jax.random.fold_in(own_key, 6), axis_at), (shards_of,), jnp.float32, low / len(pieces), top_value / len(pieces))
        return jnp.repeat(jnp.exp(steps), shape[axis_at] // shards_of).reshape((-1,) + (1,) * (len(shape) - axis_at - 1))

    factor_of = one(*pieces[0])
    for cut in pieces[1:]:
        factor_of = factor_of * one(*cut)
    return factor_of


def routed_block(stream_key, own, number, rows, count, top, reach, slope):
    order = jax.random.permutation(stream_key, count)
    crowded, common = shares(count, rows * top, reach, slope, True), shares(count, rows * top, reach, slope, False)
    places = jnp.arange(count)

    def named(tallies, turn):
        used = int((tallies > 0).sum())
        fixed = max(1, used // 4)
        moved = fixed + (places - fixed + turn * (used - fixed)) % max(1, count - fixed)
        return jnp.zeros((count,), jnp.int32).at[order[jnp.where(places < fixed, places, moved)]].set(jnp.asarray(tallies, jnp.int32))

    tallies = jnp.where(number % 4 == 0, named(crowded, number // 4), named(common, number - number // 4 - 1))
    mixed = jax.random.permutation(jax.random.fold_in(own, 3), count)
    source_of, sink = mixed[0:count // 2 * 2:2], mixed[1:count // 2 * 2:2]
    margin = jnp.minimum(tallies[source_of] - 1, reach - tallies[sink]) // 2
    margin = jnp.where((source_of == order[0]) | (sink == order[0]) | (tallies[sink] == 0), 0, jnp.maximum(margin, 0))
    moved = jax.random.randint(jax.random.fold_in(own, 4), (count // 2,), 0, 1 << 20) % (margin + 1)
    tallies = tallies.at[source_of].add(-moved).at[sink].add(moved)
    items = jnp.searchsorted(jnp.cumsum(tallies), jnp.arange(rows * top), side="right").astype(jnp.int32)
    listing = items.reshape(top, rows).T
    listing = listing[jax.random.permutation(jax.random.fold_in(own, 1), rows)]
    turn = jax.random.randint(jax.random.fold_in(own, 2), (rows, 1), 0, top)
    return jnp.take_along_axis(listing, (jnp.arange(top)[None, :] + turn) % top, axis=1)


def shares(number_of, total, most, skew, full):
    loads = [(1 << 20) // math.isqrt(standing ** skew) + 1 for standing in range(1, number_of + 1)]
    largest = most if full else min(most, max(-(-total // number_of), total * loads[0] // sum(loads)))
    least = 1 if total - largest >= number_of - 1 else 0
    given, surplus = [largest] + [least] * (number_of - 1), total - largest - least * (number_of - 1)
    while surplus > 0:
        movable = [i for i in range(1, number_of) if given[i] < largest] or [i for i in range(1, number_of) if given[i] < most]
        whole, remaining = sum([loads[i] for i in movable]), surplus
        for i in movable:
            more = min(most - given[i], max(1, remaining * loads[i] // whole), surplus)
            given[i] = given[i] + more
            surplus = surplus - more
    return np.array(given)


def noise(rng, dims, spread, limit, cuts=(), held_as=jnp.bfloat16):
    entries = spread * jax.random.normal(rng, dims, jnp.float32)
    if cuts:
        entries = entries * steps_of(rng, dims, cuts, -0.22, 0.18)
    return jnp.clip(entries, -limit, limit).astype(held_as)


def setup_inputs(seed: int = 0) -> dict:
    keys = jax.random.split(jax.random.key(seed), 6)
    crm_state = noise(keys[0], (F, NZ, NX, COLUMNS), 1.0, 6.0, ((3, 128),), jnp.float32)
    gcm_state = noise(keys[1], (F, NZ, EXT, EYT, NP, NP), 1.0, 6.0, ((2, 16), (3, 8)), jnp.float32)
    mass = jnp.clip(jnp.exp(math.log(2.0) - 1.3862944 * jax.random.uniform(keys[2], (NZ, EXT, EYT, NP, NP), jnp.float32) ** steps_of(keys[2], (NZ, EXT, EYT, NP, NP), ((1, 16), (2, 8)), -0.2, 0.2)), 0.5, 2.0)
    dest_keys = jax.random.split(jax.random.fold_in(keys[3], 1), COLUMNS // COL_DEV)
    dest_turns = jax.random.permutation(jax.random.fold_in(keys[3], 3), COLUMNS // COL_DEV)
    dest = jax.vmap(lambda own, number: routed_block(jax.random.fold_in(keys[3], 2), own, number, COL_DEV, DEVICES, 1, CAP, 2))(dest_keys, dest_turns).reshape((COLUMNS, 1))
    cost_class = with_ends(jax.random.randint(keys[4], (COLUMNS,), 1, 3), jax.random.fold_in(keys[4], 1), 1, 2).astype(jnp.int32)
    return {"crm_state": crm_state, "gcm_state": gcm_state, "mass": mass, "dest": dest, "cost_class": cost_class}


diffusion = 0.1
advection = 0.15
buoyancy = 0.3
latent_heat = 0.5
fallout = 0.2
condense_rate = 0.4
nudging = 0.5


def neighbours(values):
    eastward = jnp.roll(values, -1, axis=1)
    westward = jnp.roll(values, 1, axis=1)
    bottom = jnp.zeros_like(values[:1])
    upward = jnp.concatenate([values[1:], bottom], axis=0)
    downward = jnp.concatenate([bottom, values[:-1]], axis=0)
    return eastward, westward, upward, downward


def substep(fields, profiles):
    column_mean = jnp.mean(fields, axis=2)
    nudged = nudging * (profiles - column_mean)
    x_wind = fields[0]
    condensed = condense_rate * jax.nn.relu(fields[3])
    changes = []
    for number in range(5):
        values = fields[number]
        eastward, westward, upward, downward = neighbours(values)
        change = diffusion * (eastward + westward + upward + downward - 4.0 * values)
        change = change - advection * 0.5 * x_wind * (eastward - westward) + nudged[number][:, None, :]
        changes.append(change)
    changes[1] = changes[1] + buoyancy * fields[2]
    changes[2] = changes[2] - buoyancy * fields[1] + latent_heat * condensed
    changes[3] = changes[3] - condensed
    changes[4] = changes[4] + condensed - fallout * fields[4]
    return fields + jnp.stack(changes)


def cloud_run(fields, profiles, substeps):
    after_one = jnp.where(substeps >= 1.0, substep(fields, profiles), fields)
    return jnp.where(substeps >= 2.0, substep(after_one, profiles), after_one)


def edge_sum(weighted):
    east_x = weighted[:, :, :, :, NP - 1, :]
    west_x = weighted[:, :, :, :, 0, :]
    weighted = weighted.at[:, :, :, :, NP - 1, :].add(jnp.roll(west_x, -1, axis=2))
    weighted = weighted.at[:, :, :, :, 0, :].add(jnp.roll(east_x, 1, axis=2))
    north_face = weighted[:, :, :, :, :, NP - 1]
    south_face = weighted[:, :, :, :, :, 0]
    weighted = weighted.at[:, :, :, :, :, NP - 1].add(jnp.roll(south_face, -1, axis=3))
    weighted = weighted.at[:, :, :, :, :, 0].add(jnp.roll(north_face, 1, axis=3))
    return weighted


def to_columns(element_grid):
    blocked = element_grid.reshape(F, NZ, N_EX, ELX, N_EY, ELY, NP, NP)
    return blocked.transpose(0, 1, 2, 4, 3, 5, 6, 7).reshape(F, NZ, COLUMNS)


def from_columns(by_column):
    blocked = by_column.reshape(F, NZ, N_EX, N_EY, ELX, ELY, NP, NP)
    return blocked.transpose(0, 1, 2, 4, 3, 5, 6, 7).reshape(F, NZ, EXT, EYT, NP, NP)


def reference(crm_state, gcm_state, mass, dest, cost_class):
    profiles = to_columns(gcm_state)
    substeps = cost_class.astype(jnp.float32)
    updated = cloud_run(crm_state, profiles, substeps)
    tendency = jnp.mean(updated - crm_state, axis=2)
    advanced = gcm_state + from_columns(tendency)
    weighted = jnp.concatenate([advanced * mass[None], mass[None]], axis=0)
    summed = edge_sum(weighted)
    gcm_out = summed[:F] / summed[F:]
    targets = dest[:, 0].astype(jnp.int32)
    onehot = (targets[:, None] == jnp.arange(DEVICES, dtype=jnp.int32)[None, :]).astype(jnp.int32)
    onehot = onehot.reshape(DEVICES, COL_DEV, DEVICES)
    earlier = (jnp.cumsum(onehot, axis=1).astype(jnp.int32) - onehot)
    ranks = jnp.sum(earlier * onehot, axis=2).astype(jnp.int32).reshape(COLUMNS)
    blocks = jnp.arange(COLUMNS, dtype=jnp.int32) // COL_DEV
    slots = (targets * SLOTS + ranks * DEVICES + blocks).astype(jnp.int32)
    cloud_slots = jnp.zeros((F, NZ, NX, DEVICES * SLOTS), jnp.float32).at[:, :, :, slots].set(updated)
    return cloud_slots, gcm_out
```

```python
import functools
import random

import jax
import jax.numpy as jnp
from jax import lax
from jax.experimental import pallas as pl
from jax.experimental.pallas import tpu as pltpu
from jax.sharding import PartitionSpec as P

MESH = pl.DeviceIdType.MESH
HIGHEST = lax.Precision.HIGHEST
FIELDS, LEVELS, WIDTH, OWNED, DEVICES = 5, 12, 32, 128, 128
N_EX, N_EY = 16, 8
HALO_ROWS = 80
HALOS = (
    (0, 8, -1, 0),
    (8, 8, 1, 0),
    (16, 16, 0, -1),
    (32, 16, 0, 1),
    (48, 8, -1, -1),
    (56, 8, -1, 1),
    (64, 8, 1, -1),
    (72, 8, 1, 1),
)


def far_first():
    steps = [
        (dx, dy, dz, dc)
        for dx in range(4)
        for dy in range(4)
        for dz in range(4)
        for dc in range(2)
    ][1:]
    random.Random(0).shuffle(steps)
    return sorted(steps, key=lambda s: -sum(min(v, 4 - v) for v in s[:3]))


STEPS = far_first()


def nt_dot(a, b, precision=None):
    return lax.dot_general(
        a, b, (((1,), (1,)), ((), ())), precision=precision, preferred_element_type=jnp.float32
    )


def tn_dot(a, b, precision=None):
    return lax.dot_general(
        a, b, (((0,), (0,)), ((), ())), precision=precision, preferred_element_type=jnp.float32
    )


def level_step(source, z, profiles):
    values = [source[f, z + 1] for f in range(FIELDS)]
    drift = 0.075 * values[0]
    condensed = 0.4 * jnp.maximum(values[3], 0.0)
    after = []
    for f in range(FIELDS):
        s = values[f]
        east = pltpu.roll(s, WIDTH - 1, 0)
        west = pltpu.roll(s, 1, 0)
        nudged = 0.5 * (profiles[pl.ds(f * LEVELS + z, 1), :] - jnp.mean(s, axis=0, keepdims=True))
        change = 0.1 * (east + west + source[f, z + 2] + source[f, z] - 4.0 * s)
        change = change - drift * (east - west) + nudged
        if f == 1:
            change = change + 0.3 * values[2]
        elif f == 2:
            change = change - 0.3 * values[1] + 0.5 * condensed
        elif f == 3:
            change = change - condensed
        elif f == 4:
            change = change + condensed - 0.2 * s
        after.append(s + change)
    return values, after


def cloud_kernel(
    crm, gcm, mass, dest, cost, landed, gcm_out,
    start, first, second, profiles, weighted, faces, halo, outgoing,
    load_sem, own_sem, send_sem, recv_sem, face_send, face_recv,
):
    ex, ey = lax.axis_index("ex"), lax.axis_index("ey")
    me = ex * N_EY + ey
    px, pz, py, pc = ex // 4, ex % 4, ey // 2, ey % 2

    def peer(step):
        dx, dy, dz, dc = step
        return (
            ((px + dx) % 4) * 4 + (pz + dz) % 4,
            ((py + dy) % 4) * 2 + (pc + dc) % 2,
        )

    load = pltpu.make_async_copy(crm, start.at[:, pl.ds(1, LEVELS)], load_sem)
    load.start()
    barrier = pltpu.get_barrier_semaphore()
    for step in STEPS:
        pl.semaphore_signal(barrier, inc=1, device_id=peer(step), device_id_type=MESH)

    row = lax.broadcasted_iota(jnp.int32, (OWNED, OWNED), 0)
    lane = lax.broadcasted_iota(jnp.int32, (OWNED, OWNED), 1)
    target = dest[...].astype(jnp.float32)
    target_rows = jnp.sum(jnp.where(row == lane, target, 0.0), axis=1, keepdims=True)
    earlier = jnp.where((target_rows == target) & (row < lane), 1.0, 0.0)
    slot = jnp.sum(earlier, axis=0, keepdims=True) * DEVICES + target
    slots = lax.broadcasted_iota(jnp.int32, (2 * DEVICES, OWNED), 0).astype(jnp.float32)
    chosen = jnp.where(slots == slot, 1.0, 0.0).astype(jnp.bfloat16)

    for f in range(FIELDS):
        profiles[f * LEVELS:(f + 1) * LEVELS, :] = jnp.swapaxes(gcm[f], 0, 1)
    mass_rows = jnp.swapaxes(mass[...], 0, 1)

    zero = jnp.zeros((WIDTH, OWNED), jnp.float32)
    for f in range(FIELDS):
        for z in (0, LEVELS + 1):
            start[f, z] = zero
            first[f, z] = zero
    load.wait()
    substeps = cost[...].astype(jnp.float32)
    once, twice = substeps >= 1.0, substeps >= 2.0

    @pl.loop(0, LEVELS)
    def _(z):
        values, after = level_step(start, z, profiles)
        for f in range(FIELDS):
            first[f, z + 1] = jnp.where(once, after[f], values[f])

    @pl.loop(0, LEVELS)
    def _(z):
        values, after = level_step(first, z, profiles)
        for f in range(FIELDS):
            updated = jnp.where(twice, after[f], values[f])
            second[f, z] = updated
            tendency = jnp.mean(updated - start[f, z + 1], axis=0, keepdims=True)
            weighted[pl.ds(f * LEVELS + z, 1), :] = tendency

    for r in range(2):
        outgoing[pl.ds(r * 16 + 15, DEVICES, stride=32), :] = jnp.zeros((DEVICES, 128), jnp.float32)

    @pl.loop(0, FIELDS)
    def _(f):
        for part in range(3):
            block = second[f, 4 * part:4 * part + 4].reshape(128, OWNED)
            high = block.astype(jnp.bfloat16)
            rest = block - high.astype(jnp.float32)
            middle = rest.astype(jnp.bfloat16)
            low = (rest - middle.astype(jnp.float32)).astype(jnp.bfloat16)
            moved = nt_dot(chosen, high) + nt_dot(chosen, middle) + nt_dot(chosen, low)
            for r in range(2):
                outgoing[pl.ds(f * 3 + part + r * 16, DEVICES, stride=32), :] = moved[
                    r * DEVICES:(r + 1) * DEVICES
                ]

    for f in range(FIELDS):
        rows = slice(f * LEVELS, (f + 1) * LEVELS)
        weighted[rows, :] = (weighted[rows, :] + profiles[rows, :]) * mass_rows
    weighted[60:72, :] = mass_rows
    weighted[72:128, :] = jnp.zeros((56, OWNED), jnp.float32)
    hrow = lax.broadcasted_iota(jnp.int32, (HALO_ROWS, OWNED), 0)
    hlane = lax.broadcasted_iota(jnp.int32, (HALO_ROWS, OWNED), 1)
    x_node = (hrow % 8 // 4) * 16 + hrow % 4
    y_node = ((hrow % 16) // 4) * 32 + (hrow % 4) * 4
    node = jnp.where(hrow < 8, x_node, x_node + 108)
    node = jnp.where(hrow < 16, node, jnp.where(hrow < 32, y_node, y_node + 19))
    corner = jnp.where(hrow == 48, 0, jnp.where(hrow == 56, 19, jnp.where(hrow == 64, 108, 127)))
    corner = jnp.where(hrow % 8 == 0, corner, -1)
    node = jnp.where(hrow < 48, node, corner)
    faces[...] = nt_dot(jnp.where(node == hlane, 1.0, 0.0), weighted[...], HIGHEST)

    pl.semaphore_wait(barrier, DEVICES - 1)
    face_copies = []
    for i, (at, rows, sx, sy) in enumerate(HALOS):
        copy = pltpu.make_async_remote_copy(
            src_ref=faces.at[pl.ds(at, rows)],
            dst_ref=halo.at[pl.ds(at, rows)],
            send_sem=face_send.at[i],
            recv_sem=face_recv.at[i],
            device_id=((ex + sx + N_EX) % N_EX, (ey + sy + N_EY) % N_EY),
            device_id_type=MESH,
        )
        copy.start()
        face_copies.append(copy)
    copies = []
    mine = pl.ds(pl.multiple_of(me * 32, 32), 32)
    for i, step in enumerate(STEPS):
        at_ex, at_ey = peer(step)
        there = pl.ds(pl.multiple_of((at_ex * N_EY + at_ey) * 32, 32), 32)
        copy = pltpu.make_async_remote_copy(
            src_ref=outgoing.at[there],
            dst_ref=landed.at[mine],
            send_sem=send_sem.at[i],
            recv_sem=recv_sem.at[i],
            device_id=(at_ex, at_ey),
            device_id_type=MESH,
        )
        copy.start()
        copies.append(copy)
    own = pltpu.make_async_copy(outgoing.at[mine], landed.at[mine], own_sem)
    own.start()

    def place(index):
        across = (index // 32) * 3 + index % 16 // 4
        along = (index // 16 % 2) * 3 + index % 4
        return across * 8 + along

    for copy in face_copies:
        copy.wait()
    shared = jnp.where(place(row) == place(lane), 1.0, 0.0)
    hside = jnp.where(hrow < 8, 96, 0) + (hrow % 8 // 4) * 3 + hrow % 4
    hfront = ((hrow % 16 // 4) * 3 + hrow % 4) * 8 + jnp.where(hrow < 32, 6, 0)
    hcorner = jnp.where(
        hrow == 48, 102, jnp.where(hrow == 56, 96, jnp.where(hrow == 64, 6, 0))
    )
    hcorner = jnp.where(hrow % 8 == 0, hcorner, -1)
    hplace = jnp.where(hrow < 16, hside, jnp.where(hrow < 48, hfront, hcorner))
    met = jnp.where(hplace == place(hlane), 1.0, 0.0)
    summed = jnp.dot(weighted[...], shared, precision=HIGHEST, preferred_element_type=jnp.float32)
    summed = summed + tn_dot(halo[...], met, HIGHEST)
    below = summed[60:72]
    for f in range(FIELDS):
        gcm_out[f] = jnp.swapaxes(summed[f * LEVELS:(f + 1) * LEVELS] / below, 0, 1)

    own.wait()
    for copy in copies:
        copy.wait()


def unpack_kernel(landed, gcm_in, cloud, gcm_out, held, laid, in_sem, out_sem):
    load = pltpu.make_async_copy(landed, held, in_sem)
    load.start()
    gcm_out[...] = gcm_in[...]
    load.wait()
    copies = []
    for f in range(FIELDS):
        for part in range(3):
            at = (f * 3 + part) * 128
            for r in range(2):
                block = held[pl.ds(f * 3 + part + r * 16, DEVICES, stride=32), :]
                laid[at:at + 128, r * 128:(r + 1) * 128] = block.T
        rows = pl.ds(f * 384, 384)
        copy = pltpu.make_async_copy(laid.at[rows], cloud.at[rows], out_sem.at[f])
        copy.start()
        copies.append(copy)
    for copy in copies:
        copy.wait()


def body(crm_state, gcm_state, mass, dest, cost_class):
    any_space = pl.BlockSpec(memory_space=pl.ANY)
    vmem = pl.BlockSpec(memory_space=pltpu.VMEM)
    gcm_rows = gcm_state.transpose(0, 2, 3, 4, 5, 1).reshape(FIELDS, OWNED, LEVELS)
    mass_rows = mass.transpose(1, 2, 3, 4, 0).reshape(OWNED, LEVELS)
    landed, gcm_out = pl.pallas_call(
        cloud_kernel,
        out_shape=(
            jax.ShapeDtypeStruct((DEVICES * 32, 128), jnp.float32),
            jax.ShapeDtypeStruct((FIELDS, OWNED, LEVELS), jnp.float32),
        ),
        in_specs=[any_space, vmem, vmem, vmem, vmem],
        out_specs=(any_space, vmem),
        scratch_shapes=[
            pltpu.VMEM((FIELDS, LEVELS + 2, WIDTH, OWNED), jnp.float32),
            pltpu.VMEM((FIELDS, LEVELS + 2, WIDTH, OWNED), jnp.float32),
            pltpu.VMEM((FIELDS, LEVELS, WIDTH, OWNED), jnp.float32),
            pltpu.VMEM((FIELDS * LEVELS, OWNED), jnp.float32),
            pltpu.VMEM((128, OWNED), jnp.float32),
            pltpu.VMEM((HALO_ROWS, 128), jnp.float32),
            pltpu.VMEM((HALO_ROWS, 128), jnp.float32),
            pltpu.VMEM((DEVICES * 32, 128), jnp.float32),
            pltpu.SemaphoreType.DMA,
            pltpu.SemaphoreType.DMA,
            pltpu.SemaphoreType.DMA((DEVICES - 1,)),
            pltpu.SemaphoreType.DMA((DEVICES - 1,)),
            pltpu.SemaphoreType.DMA((8,)),
            pltpu.SemaphoreType.DMA((8,)),
        ],
        compiler_params=pltpu.CompilerParams(
            collective_id=0, has_side_effects=True, vmem_limit_bytes=48 * 2**20
        ),
        name="clouds",
    )(crm_state, gcm_rows, mass_rows, dest.reshape(1, OWNED), cost_class.reshape(1, OWNED))
    cloud, gcm_out = pl.pallas_call(
        unpack_kernel,
        out_shape=(
            jax.ShapeDtypeStruct((FIELDS * LEVELS * WIDTH, 2 * DEVICES), jnp.float32),
            jax.ShapeDtypeStruct((FIELDS, OWNED, LEVELS), jnp.float32),
        ),
        in_specs=[any_space, vmem],
        out_specs=(any_space, vmem),
        scratch_shapes=[
            pltpu.VMEM((DEVICES * 32, 128), jnp.float32),
            pltpu.VMEM((FIELDS * LEVELS * WIDTH, 2 * DEVICES), jnp.float32),
            pltpu.SemaphoreType.DMA,
            pltpu.SemaphoreType.DMA((FIELDS,)),
        ],
        compiler_params=pltpu.CompilerParams(vmem_limit_bytes=48 * 2**20),
        name="unpack",
    )(landed, gcm_out)
    cloud = cloud.reshape(FIELDS, LEVELS, WIDTH, 2 * DEVICES)
    gcm_out = gcm_out.reshape(FIELDS, 4, 2, 4, 4, LEVELS).transpose(0, 5, 1, 2, 3, 4)
    return cloud, gcm_out


def solution(mesh):
    return jax.shard_map(
        body,
        mesh=mesh,
        in_specs=(
            P(None, None, None, ("ex", "ey")),
            P(None, None, "ex", "ey", None, None),
            P(None, "ex", "ey", None, None),
            P(("ex", "ey"), None),
            P(("ex", "ey")),
        ),
        out_specs=(P(None, None, None, ("ex", "ey")), P(None, None, "ex", "ey", None, None)),
        check_vma=False,
    )
```

```python
import functools
import random

import jax
import jax.numpy as jnp
from jax import lax
from jax.experimental import pallas as pl
from jax.experimental.pallas import tpu as pltpu
from jax.sharding import PartitionSpec as P

MESH = pl.DeviceIdType.MESH
HIGHEST = lax.Precision.HIGHEST
FIELDS, LEVELS, WIDTH, OWNED, DEVICES = 5, 12, 32, 128, 128
N_EX, N_EY = 16, 8
HALO_ROWS = 80
PIECE = 10
PART_ROWS = DEVICES * PIECE
HALOS = (
    (0, 8, -1, 0),
    (8, 8, 1, 0),
    (16, 16, 0, -1),
    (32, 16, 0, 1),
    (48, 8, -1, -1),
    (56, 8, -1, 1),
    (64, 8, 1, -1),
    (72, 8, 1, 1),
)


def far_first():
    steps = [
        (dx, dy, dz, dc)
        for dx in range(4)
        for dy in range(4)
        for dz in range(4)
        for dc in range(2)
    ][1:]
    random.Random(0).shuffle(steps)
    return sorted(steps, key=lambda s: -sum(min(v, 4 - v) for v in s[:3]))


STEPS = far_first()


def nt_dot(a, b, precision=None):
    return lax.dot_general(
        a, b, (((1,), (1,)), ((), ())), precision=precision, preferred_element_type=jnp.float32
    )


def tn_dot(a, b, precision=None):
    return lax.dot_general(
        a, b, (((0,), (0,)), ((), ())), precision=precision, preferred_element_type=jnp.float32
    )


def level_step(source, z, profiles, means):
    values = [source[f, z + 1, 8:40] for f in range(FIELDS)]
    drift = 0.075 * values[0]
    condensed = 0.4 * jnp.maximum(values[3], 0.0)
    after = []
    for f in range(FIELDS):
        s = values[f]
        west, east = source[f, z + 1, 7:39], source[f, z + 1, 9:41]
        mean = jnp.sum(s, axis=0, keepdims=True) * (1.0 / WIDTH)
        if means is not None:
            means[pl.ds(f * LEVELS + z, 1), :] = mean
        nudged = 0.5 * (profiles[pl.ds(f * LEVELS + z, 1), :] - mean)
        near = (east + west) + (source[f, z + 2, 8:40] + source[f, z, 8:40])
        kept = 0.4 if f == 4 else 0.6
        new = (kept * s + 0.1 * near) - drift * (east - west) + nudged
        if f == 1:
            new = new + 0.3 * values[2]
        elif f == 2:
            new = new - 0.3 * values[1] + 0.5 * condensed
        elif f == 3:
            new = new - condensed
        elif f == 4:
            new = new + condensed
        after.append(new)
    return values, after


def cloud_kernel(
    crm, gcm_hbm, mass_hbm, dest_hbm, cost_hbm, landed, gcm_out,
    start, first, second, profiles, means, weighted, faces, halo, outgoing,
    gcm, gcm_new, mass, dest, cost, load_sem, own_sem, send_sem, recv_sem, face_send, face_recv,
):
    ex, ey = lax.axis_index("ex"), lax.axis_index("ey")
    me = ex * N_EY + ey
    px, pz, py, pc = ex // 4, ex % 4, ey // 2, ey % 2

    at_ex = [[((px + dx) % 4) * 4 + (pz + dz) % 4 for dz in range(4)] for dx in range(4)]
    at_ey = [[((py + dy) % 4) * 2 + (pc + dc) % 2 for dc in range(2)] for dy in range(4)]

    def peer(step):
        dx, dy, dz, dc = step
        return at_ex[dx][dz], at_ey[dy][dc]

    loads = [
        pltpu.make_async_copy(source, into, load_sem.at[i])
        for i, (source, into) in enumerate(
            (
                (dest_hbm, dest),
                (gcm_hbm, gcm),
                (mass_hbm, mass),
                (cost_hbm, cost),
                (crm, start.at[:, pl.ds(1, LEVELS), pl.ds(8, WIDTH)]),
                (crm.at[:, :, pl.ds(WIDTH - 1, 1)], start.at[:, pl.ds(1, LEVELS), pl.ds(7, 1)]),
                (crm.at[:, :, pl.ds(0, 1)], start.at[:, pl.ds(1, LEVELS), pl.ds(40, 1)]),
            )
        )
    ]
    for load in loads:
        load.start()
    barrier = pltpu.get_barrier_semaphore()
    for step in STEPS:
        pl.semaphore_signal(barrier, inc=1, device_id=peer(step), device_id_type=MESH)

    loads[0].wait()
    row = lax.broadcasted_iota(jnp.int32, (OWNED, OWNED), 0)
    lane = lax.broadcasted_iota(jnp.int32, (OWNED, OWNED), 1)
    target = dest[...].astype(jnp.float32)
    target_rows = jnp.sum(jnp.where(row == lane, target, 0.0), axis=1, keepdims=True)
    earlier = jnp.where((target_rows == target) & (row < lane), 1.0, 0.0)
    slot = jnp.sum(earlier, axis=0, keepdims=True) * DEVICES + target
    slots = lax.broadcasted_iota(jnp.int32, (2 * DEVICES, OWNED), 0).astype(jnp.float32)
    chosen = jnp.where(slots == slot, 1.0, 0.0).astype(jnp.bfloat16)

    loads[1].wait()
    loads[2].wait()
    for f in range(FIELDS):
        profiles[f * LEVELS:(f + 1) * LEVELS, :] = jnp.swapaxes(gcm[f], 0, 1)
    mass_rows = jnp.swapaxes(mass[...], 0, 1)

    zero = jnp.zeros((WIDTH, OWNED), jnp.float32)
    for f in range(FIELDS):
        for z in (0, LEVELS + 1):
            start[f, z, 8:40] = zero
            first[f, z, 8:40] = zero
    for load in loads[3:]:
        load.wait()
    twice = cost[...].astype(jnp.float32) >= 2.0

    chosen_pair = jnp.concatenate([chosen, chosen], axis=1)

    def advance_once(first_level, last_level):
        @pl.loop(first_level, last_level)
        def _(z):
            _, after = level_step(start, z, profiles, means)
            for f in range(FIELDS):
                first[f, z + 1, 8:40] = after[f]
                first[f, z + 1, 7:8] = after[f][WIDTH - 1:]
                first[f, z + 1, 40:41] = after[f][:1]

    def advance_twice(first_level, last_level):
        @pl.loop(first_level, last_level, unroll=2)
        def _(z):
            values, after = level_step(first, z, profiles, None)
            for f in range(FIELDS):
                updated = jnp.where(twice, after[f], values[f])
                second[f, z] = updated
                at = pl.ds(f * LEVELS + z, 1)
                mean = jnp.sum(updated, axis=0, keepdims=True) * (1.0 / WIDTH)
                weighted[at, :] = mean - means[at, :]

    def select(part):
        for f in range(FIELDS):
            block = second[f, 4 * part:4 * part + 4].reshape(128, OWNED)
            high = block.astype(jnp.bfloat16)
            low = (block - high.astype(jnp.float32)).astype(jnp.bfloat16)
            moved = nt_dot(chosen_pair, jnp.concatenate([high, low], axis=1))
            for r in range(2):
                at = part * PART_ROWS + r * FIELDS + f
                outgoing[pl.ds(at, DEVICES, stride=PIECE), :] = moved[
                    r * DEVICES:(r + 1) * DEVICES
                ]

    def send(part):
        mine = pl.ds(part * PART_ROWS + me * PIECE, PIECE)
        for step in STEPS:
            there_ex, there_ey = peer(step)
            there = pl.ds(part * PART_ROWS + (there_ex * N_EY + there_ey) * PIECE, PIECE)
            pltpu.make_async_remote_copy(
                src_ref=outgoing.at[there],
                dst_ref=landed.at[mine],
                send_sem=send_sem,
                recv_sem=recv_sem,
                device_id=(there_ex, there_ey),
                device_id_type=MESH,
            ).start()
        own = pltpu.make_async_copy(outgoing.at[mine], landed.at[mine], own_sem.at[part])
        own.start()
        return own

    advance_once(0, 5)
    advance_twice(0, 4)
    select(0)
    pl.semaphore_wait(barrier, DEVICES - 1)
    owns = [send(0)]
    advance_once(5, 9)
    advance_twice(4, 8)
    select(1)
    owns.append(send(1))
    advance_once(9, 12)
    advance_twice(8, 12)
    select(2)

    for f in range(FIELDS):
        rows = slice(f * LEVELS, (f + 1) * LEVELS)
        weighted[rows, :] = (weighted[rows, :] + profiles[rows, :]) * mass_rows
    weighted[60:72, :] = mass_rows
    weighted[72:128, :] = jnp.zeros((56, OWNED), jnp.float32)
    hrow = lax.broadcasted_iota(jnp.int32, (HALO_ROWS, OWNED), 0)
    hlane = lax.broadcasted_iota(jnp.int32, (HALO_ROWS, OWNED), 1)
    x_node = (hrow % 8 // 4) * 16 + hrow % 4
    y_node = ((hrow % 16) // 4) * 32 + (hrow % 4) * 4
    node = jnp.where(hrow < 8, x_node, x_node + 108)
    node = jnp.where(hrow < 16, node, jnp.where(hrow < 32, y_node, y_node + 19))
    corner = jnp.where(hrow == 48, 0, jnp.where(hrow == 56, 19, jnp.where(hrow == 64, 108, 127)))
    corner = jnp.where(hrow % 8 == 0, corner, -1)
    node = jnp.where(hrow < 48, node, corner)
    faces[...] = nt_dot(jnp.where(node == hlane, 1.0, 0.0), weighted[...], HIGHEST)

    face_copies = []
    for i, (at, rows, sx, sy) in enumerate(HALOS):
        copy = pltpu.make_async_remote_copy(
            src_ref=faces.at[pl.ds(at, rows)],
            dst_ref=halo.at[pl.ds(at, rows)],
            send_sem=face_send.at[i],
            recv_sem=face_recv.at[i],
            device_id=((ex + sx + N_EX) % N_EX, (ey + sy + N_EY) % N_EY),
            device_id_type=MESH,
        )
        copy.start()
        face_copies.append(copy)
    owns.append(send(2))

    def place(index):
        across = (index // 32) * 3 + index % 16 // 4
        along = (index // 16 % 2) * 3 + index % 4
        return across * 8 + along

    for copy in face_copies:
        copy.wait()
    shared = jnp.where(place(row) == place(lane), 1.0, 0.0)
    hside = jnp.where(hrow < 8, 96, 0) + (hrow % 8 // 4) * 3 + hrow % 4
    hfront = ((hrow % 16 // 4) * 3 + hrow % 4) * 8 + jnp.where(hrow < 32, 6, 0)
    hcorner = jnp.where(
        hrow == 48, 102, jnp.where(hrow == 56, 96, jnp.where(hrow == 64, 6, 0))
    )
    hcorner = jnp.where(hrow % 8 == 0, hcorner, -1)
    hplace = jnp.where(hrow < 16, hside, jnp.where(hrow < 48, hfront, hcorner))
    met = jnp.where(hplace == place(hlane), 1.0, 0.0)
    summed = jnp.dot(weighted[...], shared, precision=HIGHEST, preferred_element_type=jnp.float32)
    summed = summed + tn_dot(halo[...], met, HIGHEST)
    below = summed[60:72]
    for f in range(FIELDS):
        gcm_new[f] = jnp.swapaxes(summed[f * LEVELS:(f + 1) * LEVELS] / below, 0, 1)

    store = pltpu.make_async_copy(gcm_new, gcm_out, load_sem.at[0])
    store.start()
    for own in owns:
        own.wait()
    store.wait()
    everything = pl.ds(0, 3 * (DEVICES - 1) * PIECE)
    pltpu.make_async_copy(outgoing.at[everything], outgoing.at[everything], send_sem).wait()
    pltpu.make_async_copy(landed.at[everything], landed.at[everything], recv_sem).wait()


def unpack_kernel(landed, gcm_in, cloud, gcm_out, held, gcm_held, laid, in_sem, out_sem):
    loads = []
    for part in range(3):
        rows = pl.ds(part * PART_ROWS, PART_ROWS)
        load = pltpu.make_async_copy(landed.at[rows], held.at[rows], in_sem.at[part])
        load.start()
        loads.append(load)
    gcm_load = pltpu.make_async_copy(gcm_in, gcm_held, in_sem.at[3])
    gcm_load.start()
    stores = []
    for part in range(3):
        loads[part].wait()
        for f in range(FIELDS):
            for r in range(2):
                at = part * PART_ROWS + r * FIELDS + f
                block = held[pl.ds(at, DEVICES, stride=PIECE), :]
                laid[f, part * 128:(part + 1) * 128, r * 128:(r + 1) * 128] = block.T
        rows = pl.ds(part * 128, 128)
        store = pltpu.make_async_copy(laid.at[:, rows], cloud.at[:, rows], out_sem.at[part])
        store.start()
        stores.append(store)
        if part == 0:
            gcm_load.wait()
            store = pltpu.make_async_copy(gcm_held, gcm_out, out_sem.at[3])
            store.start()
            stores.append(store)
    for store in stores:
        store.wait()


def body(crm_state, gcm_state, mass, dest, cost_class):
    any_space = pl.BlockSpec(memory_space=pl.ANY)
    gcm_rows = gcm_state.transpose(0, 2, 3, 4, 5, 1).reshape(FIELDS, OWNED, LEVELS)
    mass_rows = mass.transpose(1, 2, 3, 4, 0).reshape(OWNED, LEVELS)
    landed, gcm_out = pl.pallas_call(
        cloud_kernel,
        out_shape=(
            jax.ShapeDtypeStruct((3 * PART_ROWS, 128), jnp.float32),
            jax.ShapeDtypeStruct((FIELDS, OWNED, LEVELS), jnp.float32),
        ),
        in_specs=[pl.BlockSpec(memory_space=pltpu.HBM)] * 5,
        out_specs=(any_space, any_space),
        scratch_shapes=[
            pltpu.VMEM((FIELDS, LEVELS + 2, 48, OWNED), jnp.float32),
            pltpu.VMEM((FIELDS, LEVELS + 2, 48, OWNED), jnp.float32),
            pltpu.VMEM((FIELDS, LEVELS, WIDTH, OWNED), jnp.float32),
            pltpu.VMEM((FIELDS * LEVELS, OWNED), jnp.float32),
            pltpu.VMEM((FIELDS * LEVELS, OWNED), jnp.float32),
            pltpu.VMEM((128, OWNED), jnp.float32),
            pltpu.VMEM((HALO_ROWS, 128), jnp.float32),
            pltpu.VMEM((HALO_ROWS, 128), jnp.float32),
            pltpu.VMEM((3 * PART_ROWS, 128), jnp.float32),
            pltpu.VMEM((FIELDS, OWNED, LEVELS), jnp.float32),
            pltpu.VMEM((FIELDS, OWNED, LEVELS), jnp.float32),
            pltpu.VMEM((OWNED, LEVELS), jnp.float32),
            pltpu.VMEM((1, OWNED), jnp.int32),
            pltpu.VMEM((1, OWNED), jnp.int32),
            pltpu.SemaphoreType.DMA((7,)),
            pltpu.SemaphoreType.DMA((3,)),
            pltpu.SemaphoreType.DMA,
            pltpu.SemaphoreType.DMA,
            pltpu.SemaphoreType.DMA((8,)),
            pltpu.SemaphoreType.DMA((8,)),
        ],
        compiler_params=pltpu.CompilerParams(
            collective_id=0, has_side_effects=True, vmem_limit_bytes=67043328
        ),
        name="clouds",
    )(crm_state, gcm_rows, mass_rows, dest.reshape(1, OWNED), cost_class.reshape(1, OWNED))
    cloud, gcm_out = pl.pallas_call(
        unpack_kernel,
        out_shape=(
            jax.ShapeDtypeStruct((FIELDS, LEVELS * WIDTH, 2 * DEVICES), jnp.float32),
            jax.ShapeDtypeStruct((FIELDS, OWNED, LEVELS), jnp.float32),
        ),
        in_specs=[any_space, any_space],
        out_specs=(any_space, any_space),
        scratch_shapes=[
            pltpu.VMEM((3 * PART_ROWS, 128), jnp.float32),
            pltpu.VMEM((FIELDS, OWNED, LEVELS), jnp.float32),
            pltpu.VMEM((FIELDS, LEVELS * WIDTH, 2 * DEVICES), jnp.float32),
            pltpu.SemaphoreType.DMA((4,)),
            pltpu.SemaphoreType.DMA((4,)),
        ],
        compiler_params=pltpu.CompilerParams(vmem_limit_bytes=67043328),
        name="unpack",
    )(landed, gcm_out)
    cloud = cloud.reshape(FIELDS, LEVELS, WIDTH, 2 * DEVICES)
    gcm_out = gcm_out.reshape(FIELDS, 4, 2, 4, 4, LEVELS).transpose(0, 5, 1, 2, 3, 4)
    return cloud, gcm_out


def solution(mesh):
    return jax.shard_map(
        body,
        mesh=mesh,
        in_specs=(
            P(None, None, None, ("ex", "ey")),
            P(None, None, "ex", "ey", None, None),
            P(None, "ex", "ey", None, None),
            P(("ex", "ey"), None),
            P(("ex", "ey")),
        ),
        out_specs=(P(None, None, None, ("ex", "ey")), P(None, None, "ex", "ey", None, None)),
        check_vma=False,
    )
```

```python
import functools
import random

import jax
import jax.numpy as jnp
from jax import lax
from jax.experimental import pallas as pl
from jax.experimental.pallas import tpu as pltpu
from jax.sharding import PartitionSpec as P

MESH = pl.DeviceIdType.MESH
HIGHEST = lax.Precision.HIGHEST
FIELDS, LEVELS, WIDTH, OWNED, DEVICES = 5, 12, 32, 128, 128
N_EX, N_EY = 16, 8
HALO_ROWS = 80
BLOCKS = 6
BLOCK_ROWS = DEVICES * FIELDS
HALOS = (
    (0, 8, -1, 0),
    (8, 8, 1, 0),
    (16, 16, 0, -1),
    (32, 16, 0, 1),
    (48, 8, -1, -1),
    (56, 8, -1, 1),
    (64, 8, 1, -1),
    (72, 8, 1, 1),
)


def far_first():
    steps = [
        (dx, dy, dz, dc)
        for dx in range(4)
        for dy in range(4)
        for dz in range(4)
        for dc in range(2)
    ][1:]
    random.Random(0).shuffle(steps)
    return sorted(steps, key=lambda s: -sum(min(v, 4 - v) for v in s[:3]))


STEPS = far_first()
X_STEPS = [(d, 0, 0, 0) for d in (2, 1, 3)]
Y_STEPS = [(0, d, 0, 0) for d in (2, 1, 3)]
Z_STEPS = [(0, 0, d, 0) for d in (2, 1, 3)]
C_STEPS = [(0, 0, 0, 1)]
NEAR_STEPS = [s for s in STEPS if sum(v != 0 for v in s[:3]) < 2]
SIDE_STEPS = [s for s in STEPS if s not in NEAR_STEPS and 0 in s[1:3]]
FAR_STEPS = [s for s in STEPS if 0 not in s[1:3]]


def nt_dot(a, b, precision=None):
    return lax.dot_general(
        a, b, (((1,), (1,)), ((), ())), precision=precision, preferred_element_type=jnp.float32
    )


def tn_dot(a, b, precision=None):
    return lax.dot_general(
        a, b, (((0,), (0,)), ((), ())), precision=precision, preferred_element_type=jnp.float32
    )


def level_step(source, z, profiles, means):
    values = [source[f, z + 1, 8:40] for f in range(FIELDS)]
    drift = 0.075 * values[0]
    condensed = 0.4 * jnp.maximum(values[3], 0.0)
    after = []
    for f in range(FIELDS):
        s = values[f]
        west, east = source[f, z + 1, 7:39], source[f, z + 1, 9:41]
        mean = jnp.sum(s, axis=0, keepdims=True) * (1.0 / WIDTH)
        if means is not None:
            means[pl.ds(f * LEVELS + z, 1), :] = mean
        nudged = 0.5 * (profiles[pl.ds(f * LEVELS + z, 1), :] - mean)
        near = (east + west) + (source[f, z + 2, 8:40] + source[f, z, 8:40])
        kept = 0.4 if f == 4 else 0.6
        new = (kept * s + 0.1 * near) - drift * (east - west) + nudged
        if f == 1:
            new = new + 0.3 * values[2]
        elif f == 2:
            new = new - 0.3 * values[1] + 0.5 * condensed
        elif f == 3:
            new = new - condensed
        elif f == 4:
            new = new + condensed
        after.append(new)
    return values, after


def cloud_kernel(
    crm, gcm_hbm, mass_hbm, dest_hbm, cost_hbm, landed, gcm_out,
    start, first, second, profiles, means, weighted, faces, halo, outgoing,
    gcm, gcm_new, mass, dest, cost, load_sem, stage_sem, own_sem, send_sem, recv_sem, face_send, face_recv,
):
    ex, ey = lax.axis_index("ex"), lax.axis_index("ey")
    me = ex * N_EY + ey
    px, pz, py, pc = ex // 4, ex % 4, ey // 2, ey % 2

    at_ex = [[((px + dx) % 4) * 4 + (pz + dz) % 4 for dz in range(4)] for dx in range(4)]
    at_ey = [[((py + dy) % 4) * 2 + (pc + dc) % 2 for dc in range(2)] for dy in range(4)]

    def peer(step):
        dx, dy, dz, dc = step
        return at_ex[dx][dz], at_ey[dy][dc]

    loads = [
        pltpu.make_async_copy(source, into, load_sem.at[i])
        for i, (source, into) in enumerate(
            (
                (dest_hbm, dest),
                (gcm_hbm, gcm),
                (mass_hbm, mass),
                (cost_hbm, cost),
                (crm, start.at[:, pl.ds(1, LEVELS), pl.ds(8, WIDTH)]),
                (crm.at[:, :, pl.ds(WIDTH - 1, 1)], start.at[:, pl.ds(1, LEVELS), pl.ds(7, 1)]),
                (crm.at[:, :, pl.ds(0, 1)], start.at[:, pl.ds(1, LEVELS), pl.ds(40, 1)]),
            )
        )
    ]
    for load in loads:
        load.start()
    def signal(semaphore, steps):
        for step in steps:
            pl.semaphore_signal(semaphore, inc=1, device_id=peer(step), device_id_type=MESH)

    barrier = pltpu.get_barrier_semaphore()
    signal(barrier, X_STEPS + Y_STEPS + Z_STEPS + C_STEPS)

    loads[0].wait()
    row = lax.broadcasted_iota(jnp.int32, (OWNED, OWNED), 0)
    lane = lax.broadcasted_iota(jnp.int32, (OWNED, OWNED), 1)
    target = dest[...].astype(jnp.float32)
    target_rows = jnp.sum(jnp.where(row == lane, target, 0.0), axis=1, keepdims=True)
    earlier = jnp.where((target_rows == target) & (row < lane), 1.0, 0.0)
    slot = jnp.sum(earlier, axis=0, keepdims=True) * DEVICES + target
    slots = lax.broadcasted_iota(jnp.int32, (2 * DEVICES, OWNED), 0).astype(jnp.float32)
    chosen = jnp.where(slots == slot, 1.0, 0.0).astype(jnp.bfloat16)

    loads[1].wait()
    loads[2].wait()
    for f in range(FIELDS):
        profiles[f * LEVELS:(f + 1) * LEVELS, :] = jnp.swapaxes(gcm[f], 0, 1)
    mass_rows = jnp.swapaxes(mass[...], 0, 1)

    zero = jnp.zeros((WIDTH, OWNED), jnp.float32)
    for f in range(FIELDS):
        for z in (0, LEVELS + 1):
            start[f, z, 8:40] = zero
            first[f, z, 8:40] = zero
    for load in loads[3:]:
        load.wait()
    twice = cost[...].astype(jnp.float32) >= 2.0

    chosen_pair = jnp.concatenate([chosen, chosen], axis=1)

    def advance_once(first_level, last_level):
        @pl.loop(first_level, last_level)
        def _(z):
            _, after = level_step(start, z, profiles, means)
            for f in range(FIELDS):
                first[f, z + 1, 8:40] = after[f]
                first[f, z + 1, 7:8] = after[f][WIDTH - 1:]
                first[f, z + 1, 40:41] = after[f][:1]

    def advance_twice(first_level, last_level):
        @pl.loop(first_level, last_level, unroll=2)
        def _(z):
            values, after = level_step(first, z, profiles, None)
            for f in range(FIELDS):
                updated = jnp.where(twice, after[f], values[f])
                second[f, z] = updated
                at = pl.ds(f * LEVELS + z, 1)
                mean = jnp.sum(updated, axis=0, keepdims=True) * (1.0 / WIDTH)
                weighted[at, :] = mean - means[at, :]

    def select(part):
        for f in range(FIELDS):
            block = second[f, 4 * part:4 * part + 4].reshape(128, OWNED)
            high = block.astype(jnp.bfloat16)
            low = (block - high.astype(jnp.float32)).astype(jnp.bfloat16)
            moved = nt_dot(chosen_pair, jnp.concatenate([high, low], axis=1))
            for r in range(2):
                outgoing[2 * part + r, pl.ds(f, DEVICES, stride=FIELDS), :] = moved[
                    r * DEVICES:(r + 1) * DEVICES
                ]

    def piece(buffer, part, device):
        return buffer.at[pl.ds(2 * part, 2), pl.ds(device * FIELDS, FIELDS)]

    def send(part, steps):
        for step in steps:
            there_ex, there_ey = peer(step)
            pltpu.make_async_remote_copy(
                src_ref=piece(outgoing, part, there_ex * N_EY + there_ey),
                dst_ref=piece(landed, part, me),
                send_sem=send_sem,
                recv_sem=recv_sem,
                device_id=(there_ex, there_ey),
                device_id_type=MESH,
            ).start()

    pl.semaphore_wait(barrier, 10)
    signal(stage_sem.at[0], C_STEPS)
    advance_once(0, 5)
    pl.semaphore_wait(stage_sem.at[0], 1)
    signal(stage_sem.at[1], X_STEPS)
    advance_twice(0, 4)
    select(0)
    send(0, NEAR_STEPS)
    pl.semaphore_wait(stage_sem.at[1], 3)
    signal(stage_sem.at[2], Y_STEPS)
    send(0, SIDE_STEPS)
    advance_once(5, 9)
    advance_twice(4, 8)
    select(1)
    send(1, NEAR_STEPS + SIDE_STEPS)
    pl.semaphore_wait(stage_sem.at[2], 3)
    send(0, FAR_STEPS)
    send(1, FAR_STEPS)
    advance_once(9, 12)
    advance_twice(8, 12)
    select(2)

    for f in range(FIELDS):
        rows = slice(f * LEVELS, (f + 1) * LEVELS)
        weighted[rows, :] = (weighted[rows, :] + profiles[rows, :]) * mass_rows
    weighted[60:72, :] = mass_rows
    weighted[72:128, :] = jnp.zeros((56, OWNED), jnp.float32)
    hrow = lax.broadcasted_iota(jnp.int32, (HALO_ROWS, OWNED), 0)
    hlane = lax.broadcasted_iota(jnp.int32, (HALO_ROWS, OWNED), 1)
    x_node = (hrow % 8 // 4) * 16 + hrow % 4
    y_node = ((hrow % 16) // 4) * 32 + (hrow % 4) * 4
    node = jnp.where(hrow < 8, x_node, x_node + 108)
    node = jnp.where(hrow < 16, node, jnp.where(hrow < 32, y_node, y_node + 19))
    corner = jnp.where(hrow == 48, 0, jnp.where(hrow == 56, 19, jnp.where(hrow == 64, 108, 127)))
    corner = jnp.where(hrow % 8 == 0, corner, -1)
    node = jnp.where(hrow < 48, node, corner)
    faces[...] = nt_dot(jnp.where(node == hlane, 1.0, 0.0), weighted[...], HIGHEST)

    face_copies = []
    for i, (at, rows, sx, sy) in enumerate(HALOS):
        copy = pltpu.make_async_remote_copy(
            src_ref=faces.at[pl.ds(at, rows)],
            dst_ref=halo.at[pl.ds(at, rows)],
            send_sem=face_send.at[i],
            recv_sem=face_recv.at[i],
            device_id=((ex + sx + N_EX) % N_EX, (ey + sy + N_EY) % N_EY),
            device_id_type=MESH,
        )
        copy.start()
        face_copies.append(copy)
    send(2, STEPS)
    owns = []
    for part in range(3):
        own = pltpu.make_async_copy(
            piece(outgoing, part, me), piece(landed, part, me), own_sem.at[part]
        )
        own.start()
        owns.append(own)

    def place(index):
        across = (index // 32) * 3 + index % 16 // 4
        along = (index // 16 % 2) * 3 + index % 4
        return across * 8 + along

    for copy in face_copies:
        copy.wait()
    shared = jnp.where(place(row) == place(lane), 1.0, 0.0)
    hside = jnp.where(hrow < 8, 96, 0) + (hrow % 8 // 4) * 3 + hrow % 4
    hfront = ((hrow % 16 // 4) * 3 + hrow % 4) * 8 + jnp.where(hrow < 32, 6, 0)
    hcorner = jnp.where(
        hrow == 48, 102, jnp.where(hrow == 56, 96, jnp.where(hrow == 64, 6, 0))
    )
    hcorner = jnp.where(hrow % 8 == 0, hcorner, -1)
    hplace = jnp.where(hrow < 16, hside, jnp.where(hrow < 48, hfront, hcorner))
    met = jnp.where(hplace == place(hlane), 1.0, 0.0)
    summed = jnp.dot(weighted[...], shared, precision=HIGHEST, preferred_element_type=jnp.float32)
    summed = summed + tn_dot(halo[...], met, HIGHEST)
    below = summed[60:72]
    for f in range(FIELDS):
        gcm_new[f] = jnp.swapaxes(summed[f * LEVELS:(f + 1) * LEVELS] / below, 0, 1)

    store = pltpu.make_async_copy(gcm_new, gcm_out, load_sem.at[0])
    store.start()
    for own in owns:
        own.wait()
    store.wait()
    others = pl.ds(0, (DEVICES - 1) * FIELDS)
    pltpu.make_async_copy(outgoing.at[:, others], outgoing.at[:, others], send_sem).wait()
    pltpu.make_async_copy(landed.at[:, others], landed.at[:, others], recv_sem).wait()


def unpack_kernel(landed, gcm_in, cloud, gcm_out, laid, out_sem):
    stores = [pltpu.make_async_copy(gcm_in, gcm_out, out_sem.at[BLOCKS])]
    stores[0].start()
    for block in range(BLOCKS):
        rows, lanes = pl.ds(block // 2 * 128, 128), pl.ds(block % 2 * DEVICES, DEVICES)
        for f in range(FIELDS):
            laid[f, rows, lanes] = landed[block, pl.ds(f, DEVICES, stride=FIELDS), :].T
        store = pltpu.make_async_copy(
            laid.at[:, rows, lanes], cloud.at[:, rows, lanes], out_sem.at[block]
        )
        store.start()
        stores.append(store)
    for store in stores:
        store.wait()


def body(crm_state, gcm_state, mass, dest, cost_class):
    any_space = pl.BlockSpec(memory_space=pl.ANY)
    gcm_rows = gcm_state.transpose(0, 2, 3, 4, 5, 1).reshape(FIELDS, OWNED, LEVELS)
    mass_rows = mass.transpose(1, 2, 3, 4, 0).reshape(OWNED, LEVELS)
    landed, gcm_out = pl.pallas_call(
        cloud_kernel,
        out_shape=(
            jax.ShapeDtypeStruct((BLOCKS, BLOCK_ROWS, 128), jnp.float32),
            jax.ShapeDtypeStruct((FIELDS, OWNED, LEVELS), jnp.float32),
        ),
        in_specs=[pl.BlockSpec(memory_space=pltpu.HBM)] * 5,
        out_specs=(any_space, any_space),
        scratch_shapes=[
            pltpu.VMEM((FIELDS, LEVELS + 2, 48, OWNED), jnp.float32),
            pltpu.VMEM((FIELDS, LEVELS + 2, 48, OWNED), jnp.float32),
            pltpu.VMEM((FIELDS, LEVELS, WIDTH, OWNED), jnp.float32),
            pltpu.VMEM((FIELDS * LEVELS, OWNED), jnp.float32),
            pltpu.VMEM((FIELDS * LEVELS, OWNED), jnp.float32),
            pltpu.VMEM((128, OWNED), jnp.float32),
            pltpu.VMEM((HALO_ROWS, 128), jnp.float32),
            pltpu.VMEM((HALO_ROWS, 128), jnp.float32),
            pltpu.VMEM((BLOCKS, BLOCK_ROWS, 128), jnp.float32),
            pltpu.VMEM((FIELDS, OWNED, LEVELS), jnp.float32),
            pltpu.VMEM((FIELDS, OWNED, LEVELS), jnp.float32),
            pltpu.VMEM((OWNED, LEVELS), jnp.float32),
            pltpu.VMEM((1, OWNED), jnp.int32),
            pltpu.VMEM((1, OWNED), jnp.int32),
            pltpu.SemaphoreType.DMA((7,)),
            pltpu.SemaphoreType.REGULAR((3,)),
            pltpu.SemaphoreType.DMA((3,)),
            pltpu.SemaphoreType.DMA,
            pltpu.SemaphoreType.DMA,
            pltpu.SemaphoreType.DMA((8,)),
            pltpu.SemaphoreType.DMA((8,)),
        ],
        compiler_params=pltpu.CompilerParams(
            collective_id=0, has_side_effects=True, vmem_limit_bytes=40 * 2**20
        ),
        name="clouds",
    )(*(pltpu.with_memory_space_constraint(v, pltpu.HBM) for v in (crm_state, gcm_rows, mass_rows, dest.reshape(1, OWNED), cost_class.reshape(1, OWNED))))
    cloud, gcm_out = pl.pallas_call(
        unpack_kernel,
        out_shape=(
            jax.ShapeDtypeStruct((FIELDS, LEVELS * WIDTH, 2 * DEVICES), jnp.float32),
            jax.ShapeDtypeStruct((FIELDS, OWNED, LEVELS), jnp.float32),
        ),
        in_specs=[pl.BlockSpec(memory_space=pltpu.VMEM), pl.BlockSpec(memory_space=pltpu.VMEM)],
        out_specs=(any_space, any_space),
        scratch_shapes=[
            pltpu.VMEM((FIELDS, LEVELS * WIDTH, 2 * DEVICES), jnp.float32),
            pltpu.SemaphoreType.DMA((BLOCKS + 1,)),
        ],
        compiler_params=pltpu.CompilerParams(vmem_limit_bytes=16 * 2**20),
        name="unpack",
    )(landed, gcm_out)
    cloud = cloud.reshape(FIELDS, LEVELS, WIDTH, 2 * DEVICES)
    gcm_out = gcm_out.reshape(FIELDS, 4, 2, 4, 4, LEVELS).transpose(0, 5, 1, 2, 3, 4)
    return cloud, gcm_out


def solution(mesh):
    return jax.shard_map(
        body,
        mesh=mesh,
        in_specs=(
            P(None, None, None, ("ex", "ey")),
            P(None, None, "ex", "ey", None, None),
            P(None, "ex", "ey", None, None),
            P(("ex", "ey"), None),
            P(("ex", "ey")),
        ),
        out_specs=(P(None, None, None, ("ex", "ey")), P(None, None, "ex", "ey", None, None)),
        check_vma=False,
    )
```

```python
import functools
import random

import jax
import jax.numpy as jnp
from jax import lax
from jax.experimental import pallas as pl
from jax.experimental.pallas import tpu as pltpu
from jax.sharding import PartitionSpec as P

MESH = pl.DeviceIdType.MESH
HIGHEST = lax.Precision.HIGHEST
FIELDS, LEVELS, WIDTH, OWNED, DEVICES = 5, 12, 32, 128, 128
N_EX, N_EY = 16, 8
HALO_ROWS = 80
BLOCKS = 6
BLOCK_ROWS = DEVICES * FIELDS
HALOS = (
    (0, 8, -1, 0),
    (8, 8, 1, 0),
    (16, 16, 0, -1),
    (32, 16, 0, 1),
    (48, 8, -1, -1),
    (56, 8, -1, 1),
    (64, 8, 1, -1),
    (72, 8, 1, 1),
)


def far_first():
    steps = [
        (dx, dy, dz, dc)
        for dx in range(4)
        for dy in range(4)
        for dz in range(4)
        for dc in range(2)
    ][1:]
    random.Random(0).shuffle(steps)
    return sorted(steps, key=lambda s: -sum(min(v, 4 - v) for v in s[:3]))


STEPS = far_first()
X_STEPS = [(d, 0, 0, 0) for d in (2, 1, 3)]
Y_STEPS = [(0, d, 0, 0) for d in (2, 1, 3)]
Z_STEPS = [(0, 0, d, 0) for d in (2, 1, 3)]
C_STEPS = [(0, 0, 0, 1)]
NEAR_STEPS = [s for s in STEPS if sum(v != 0 for v in s[:3]) < 2]
SIDE_STEPS = [s for s in STEPS if s not in NEAR_STEPS and 0 in s[:3]]
FAR_STEPS = [s for s in STEPS if 0 not in s[:3]]


def nt_dot(a, b, precision=None):
    return lax.dot_general(
        a, b, (((1,), (1,)), ((), ())), precision=precision, preferred_element_type=jnp.float32
    )


def tn_dot(a, b, precision=None):
    return lax.dot_general(
        a, b, (((0,), (0,)), ((), ())), precision=precision, preferred_element_type=jnp.float32
    )


def level_step(source, z, profiles, means):
    values = [source[f, z + 1, 8:40] for f in range(FIELDS)]
    drift = 0.075 * values[0]
    condensed = 0.4 * jnp.maximum(values[3], 0.0)
    after = []
    for f in range(FIELDS):
        s = values[f]
        west, east = source[f, z + 1, 7:39], source[f, z + 1, 9:41]
        mean = jnp.sum(s, axis=0, keepdims=True) * (1.0 / WIDTH)
        if means is not None:
            means[pl.ds(f * LEVELS + z, 1), :] = mean
        nudged = 0.5 * (profiles[pl.ds(f * LEVELS + z, 1), :] - mean)
        near = (east + west) + (source[f, z + 2, 8:40] + source[f, z, 8:40])
        kept = 0.4 if f == 4 else 0.6
        new = (kept * s + 0.1 * near) - drift * (east - west) + nudged
        if f == 1:
            new = new + 0.3 * values[2]
        elif f == 2:
            new = new - 0.3 * values[1] + 0.5 * condensed
        elif f == 3:
            new = new - condensed
        elif f == 4:
            new = new + condensed
        after.append(new)
    return values, after


def cloud_kernel(
    crm, gcm_hbm, mass_hbm, dest_hbm, cost_hbm, landed, gcm_out,
    start, first, second, profiles, means, weighted, faces, halo, outgoing,
    gcm, gcm_new, mass, dest, cost, load_sem, stage_sem, own_sem, send_sem, recv_sem, face_send, face_recv,
):
    ex, ey = lax.axis_index("ex"), lax.axis_index("ey")
    me = ex * N_EY + ey
    px, pz, py, pc = ex // 4, ex % 4, ey // 2, ey % 2

    at_ex = [[((px + dx) % 4) * 4 + (pz + dz) % 4 for dz in range(4)] for dx in range(4)]
    at_ey = [[((py + dy) % 4) * 2 + (pc + dc) % 2 for dc in range(2)] for dy in range(4)]

    def peer(step):
        dx, dy, dz, dc = step
        return at_ex[dx][dz], at_ey[dy][dc]

    loads = [
        pltpu.make_async_copy(source, into, load_sem.at[i])
        for i, (source, into) in enumerate(
            (
                (dest_hbm, dest),
                (gcm_hbm, gcm),
                (mass_hbm, mass),
                (cost_hbm, cost),
                (crm, start.at[:, pl.ds(1, LEVELS), pl.ds(8, WIDTH)]),
                (crm.at[:, :, pl.ds(WIDTH - 1, 1)], start.at[:, pl.ds(1, LEVELS), pl.ds(7, 1)]),
                (crm.at[:, :, pl.ds(0, 1)], start.at[:, pl.ds(1, LEVELS), pl.ds(40, 1)]),
            )
        )
    ]
    for load in loads:
        load.start()
    def signal(semaphore, steps):
        for step in steps:
            pl.semaphore_signal(semaphore, inc=1, device_id=peer(step), device_id_type=MESH)

    barrier = pltpu.get_barrier_semaphore()
    signal(barrier, X_STEPS + Y_STEPS + Z_STEPS + C_STEPS)

    loads[0].wait()
    row = lax.broadcasted_iota(jnp.int32, (OWNED, OWNED), 0)
    lane = lax.broadcasted_iota(jnp.int32, (OWNED, OWNED), 1)
    target = dest[...].astype(jnp.float32)
    target_rows = jnp.sum(jnp.where(row == lane, target, 0.0), axis=1, keepdims=True)
    earlier = jnp.where((target_rows == target) & (row < lane), 1.0, 0.0)
    slot = jnp.sum(earlier, axis=0, keepdims=True) * DEVICES + target
    slots = lax.broadcasted_iota(jnp.int32, (2 * DEVICES, OWNED), 0).astype(jnp.float32)
    chosen = jnp.where(slots == slot, 1.0, 0.0).astype(jnp.bfloat16)

    loads[1].wait()
    loads[2].wait()
    for f in range(FIELDS):
        profiles[f * LEVELS:(f + 1) * LEVELS, :] = jnp.swapaxes(gcm[f], 0, 1)
    mass_rows = jnp.swapaxes(mass[...], 0, 1)

    zero = jnp.zeros((WIDTH, OWNED), jnp.float32)
    for f in range(FIELDS):
        for z in (0, LEVELS + 1):
            start[f, z, 8:40] = zero
            first[f, z, 8:40] = zero
    for load in loads[3:]:
        load.wait()
    twice = cost[...].astype(jnp.float32) >= 2.0

    chosen_pair = jnp.concatenate([chosen, chosen], axis=1)

    def advance_once(first_level, last_level):
        @pl.loop(first_level, last_level)
        def _(z):
            _, after = level_step(start, z, profiles, means)
            for f in range(FIELDS):
                first[f, z + 1, 8:40] = after[f]
                first[f, z + 1, 7:8] = after[f][WIDTH - 1:]
                first[f, z + 1, 40:41] = after[f][:1]

    def advance_twice(first_level, last_level):
        @pl.loop(first_level, last_level, unroll=2)
        def _(z):
            values, after = level_step(first, z, profiles, None)
            for f in range(FIELDS):
                updated = jnp.where(twice, after[f], values[f])
                second[f, z] = updated
                at = pl.ds(f * LEVELS + z, 1)
                mean = jnp.sum(updated, axis=0, keepdims=True) * (1.0 / WIDTH)
                weighted[at, :] = mean - means[at, :]

    def select(part):
        for f in range(FIELDS):
            block = second[f, 4 * part:4 * part + 4].reshape(128, OWNED)
            high = block.astype(jnp.bfloat16)
            low = (block - high.astype(jnp.float32)).astype(jnp.bfloat16)
            moved = nt_dot(chosen_pair, jnp.concatenate([high, low], axis=1))
            for r in range(2):
                outgoing[2 * part + r, pl.ds(f, DEVICES, stride=FIELDS), :] = moved[
                    r * DEVICES:(r + 1) * DEVICES
                ]

    def piece(buffer, part, device):
        return buffer.at[pl.ds(2 * part, 2), pl.ds(device * FIELDS, FIELDS)]

    def send(part, steps):
        for step in steps:
            there_ex, there_ey = peer(step)
            pltpu.make_async_remote_copy(
                src_ref=piece(outgoing, part, there_ex * N_EY + there_ey),
                dst_ref=piece(landed, part, me),
                send_sem=send_sem,
                recv_sem=recv_sem,
                device_id=(there_ex, there_ey),
                device_id_type=MESH,
            ).start()

    pl.semaphore_wait(barrier, 10)
    signal(stage_sem.at[0], C_STEPS)
    advance_once(0, 5)
    pl.semaphore_wait(stage_sem.at[0], 1)
    signal(stage_sem.at[1], X_STEPS + Y_STEPS + Z_STEPS)
    advance_twice(0, 4)
    select(0)
    send(0, NEAR_STEPS)
    pl.semaphore_wait(stage_sem.at[1], 9)
    signal(stage_sem.at[2], Y_STEPS)
    send(0, SIDE_STEPS)
    advance_once(5, 9)
    advance_twice(4, 8)
    select(1)
    send(1, NEAR_STEPS + SIDE_STEPS)
    pl.semaphore_wait(stage_sem.at[2], 3)
    send(0, FAR_STEPS)
    send(1, FAR_STEPS)
    advance_once(9, 12)
    advance_twice(8, 12)
    select(2)

    for f in range(FIELDS):
        rows = slice(f * LEVELS, (f + 1) * LEVELS)
        weighted[rows, :] = (weighted[rows, :] + profiles[rows, :]) * mass_rows
    weighted[60:72, :] = mass_rows
    weighted[72:128, :] = jnp.zeros((56, OWNED), jnp.float32)
    hrow = lax.broadcasted_iota(jnp.int32, (HALO_ROWS, OWNED), 0)
    hlane = lax.broadcasted_iota(jnp.int32, (HALO_ROWS, OWNED), 1)
    x_node = (hrow % 8 // 4) * 16 + hrow % 4
    y_node = ((hrow % 16) // 4) * 32 + (hrow % 4) * 4
    node = jnp.where(hrow < 8, x_node, x_node + 108)
    node = jnp.where(hrow < 16, node, jnp.where(hrow < 32, y_node, y_node + 19))
    corner = jnp.where(hrow == 48, 0, jnp.where(hrow == 56, 19, jnp.where(hrow == 64, 108, 127)))
    corner = jnp.where(hrow % 8 == 0, corner, -1)
    node = jnp.where(hrow < 48, node, corner)
    faces[...] = nt_dot(jnp.where(node == hlane, 1.0, 0.0), weighted[...], HIGHEST)

    face_copies = []
    for i, (at, rows, sx, sy) in enumerate(HALOS):
        copy = pltpu.make_async_remote_copy(
            src_ref=faces.at[pl.ds(at, rows)],
            dst_ref=halo.at[pl.ds(at, rows)],
            send_sem=face_send.at[i],
            recv_sem=face_recv.at[i],
            device_id=((ex + sx + N_EX) % N_EX, (ey + sy + N_EY) % N_EY),
            device_id_type=MESH,
        )
        copy.start()
        face_copies.append(copy)
    send(2, STEPS)
    owns = []
    for part in range(3):
        own = pltpu.make_async_copy(
            piece(outgoing, part, me), piece(landed, part, me), own_sem.at[part]
        )
        own.start()
        owns.append(own)

    def place(index):
        across = (index // 32) * 3 + index % 16 // 4
        along = (index // 16 % 2) * 3 + index % 4
        return across * 8 + along

    for copy in face_copies:
        copy.wait()
    shared = jnp.where(place(row) == place(lane), 1.0, 0.0)
    hside = jnp.where(hrow < 8, 96, 0) + (hrow % 8 // 4) * 3 + hrow % 4
    hfront = ((hrow % 16 // 4) * 3 + hrow % 4) * 8 + jnp.where(hrow < 32, 6, 0)
    hcorner = jnp.where(
        hrow == 48, 102, jnp.where(hrow == 56, 96, jnp.where(hrow == 64, 6, 0))
    )
    hcorner = jnp.where(hrow % 8 == 0, hcorner, -1)
    hplace = jnp.where(hrow < 16, hside, jnp.where(hrow < 48, hfront, hcorner))
    met = jnp.where(hplace == place(hlane), 1.0, 0.0)
    summed = jnp.dot(weighted[...], shared, precision=HIGHEST, preferred_element_type=jnp.float32)
    summed = summed + tn_dot(halo[...], met, HIGHEST)
    below = summed[60:72]
    for f in range(FIELDS):
        gcm_new[f] = jnp.swapaxes(summed[f * LEVELS:(f + 1) * LEVELS] / below, 0, 1)

    store = pltpu.make_async_copy(gcm_new, gcm_out, load_sem.at[0])
    store.start()
    for own in owns:
        own.wait()
    store.wait()
    others = pl.ds(0, (DEVICES - 1) * FIELDS)
    pltpu.make_async_copy(outgoing.at[:, others], outgoing.at[:, others], send_sem).wait()
    pltpu.make_async_copy(landed.at[:, others], landed.at[:, others], recv_sem).wait()


def unpack_kernel(landed, gcm_in, cloud, gcm_out, laid, out_sem):
    stores = [pltpu.make_async_copy(gcm_in, gcm_out, out_sem.at[15])]
    stores[0].start()
    for part in range(3):
        for f in range(FIELDS):
            rows = pl.ds(part * 128, 128)
            for r in range(2):
                lanes = pl.ds(r * DEVICES, DEVICES)
                laid[f, rows, lanes] = landed[2 * part + r, pl.ds(f, DEVICES, stride=FIELDS), :].T
            store = pltpu.make_async_copy(
                laid.at[f, rows], cloud.at[f, rows], out_sem.at[part * FIELDS + f]
            )
            store.start()
            stores.append(store)
    for store in stores:
        store.wait()


def body(crm_state, gcm_state, mass, dest, cost_class):
    any_space = pl.BlockSpec(memory_space=pl.ANY)
    gcm_rows = gcm_state.transpose(0, 2, 3, 4, 5, 1).reshape(FIELDS, OWNED, LEVELS)
    mass_rows = mass.transpose(1, 2, 3, 4, 0).reshape(OWNED, LEVELS)
    landed, gcm_out = pl.pallas_call(
        cloud_kernel,
        out_shape=(
            jax.ShapeDtypeStruct((BLOCKS, BLOCK_ROWS, 128), jnp.float32),
            jax.ShapeDtypeStruct((FIELDS, OWNED, LEVELS), jnp.float32),
        ),
        in_specs=[pl.BlockSpec(memory_space=pltpu.HBM)] * 5,
        out_specs=(any_space, any_space),
        scratch_shapes=[
            pltpu.VMEM((FIELDS, LEVELS + 2, 48, OWNED), jnp.float32),
            pltpu.VMEM((FIELDS, LEVELS + 2, 48, OWNED), jnp.float32),
            pltpu.VMEM((FIELDS, LEVELS, WIDTH, OWNED), jnp.float32),
            pltpu.VMEM((FIELDS * LEVELS, OWNED), jnp.float32),
            pltpu.VMEM((FIELDS * LEVELS, OWNED), jnp.float32),
            pltpu.VMEM((128, OWNED), jnp.float32),
            pltpu.VMEM((HALO_ROWS, 128), jnp.float32),
            pltpu.VMEM((HALO_ROWS, 128), jnp.float32),
            pltpu.VMEM((BLOCKS, BLOCK_ROWS, 128), jnp.float32),
            pltpu.VMEM((FIELDS, OWNED, LEVELS), jnp.float32),
            pltpu.VMEM((FIELDS, OWNED, LEVELS), jnp.float32),
            pltpu.VMEM((OWNED, LEVELS), jnp.float32),
            pltpu.VMEM((1, OWNED), jnp.int32),
            pltpu.VMEM((1, OWNED), jnp.int32),
            pltpu.SemaphoreType.DMA((7,)),
            pltpu.SemaphoreType.REGULAR((3,)),
            pltpu.SemaphoreType.DMA((3,)),
            pltpu.SemaphoreType.DMA,
            pltpu.SemaphoreType.DMA,
            pltpu.SemaphoreType.DMA((8,)),
            pltpu.SemaphoreType.DMA((8,)),
        ],
        compiler_params=pltpu.CompilerParams(
            collective_id=0, has_side_effects=True, vmem_limit_bytes=40 * 2**20
        ),
        name="clouds",
    )(*(pltpu.with_memory_space_constraint(v, pltpu.HBM) for v in (crm_state, gcm_rows, mass_rows, dest.reshape(1, OWNED), cost_class.reshape(1, OWNED))))
    cloud, gcm_out = pl.pallas_call(
        unpack_kernel,
        out_shape=(
            jax.ShapeDtypeStruct((FIELDS, LEVELS * WIDTH, 2 * DEVICES), jnp.float32),
            jax.ShapeDtypeStruct((FIELDS, OWNED, LEVELS), jnp.float32),
        ),
        in_specs=[pl.BlockSpec(memory_space=pltpu.VMEM), pl.BlockSpec(memory_space=pltpu.VMEM)],
        out_specs=(any_space, any_space),
        scratch_shapes=[
            pltpu.VMEM((FIELDS, LEVELS * WIDTH, 2 * DEVICES), jnp.float32),
            pltpu.SemaphoreType.DMA((16,)),
        ],
        compiler_params=pltpu.CompilerParams(vmem_limit_bytes=16 * 2**20),
        name="unpack",
    )(landed, gcm_out)
    cloud = cloud.reshape(FIELDS, LEVELS, WIDTH, 2 * DEVICES)
    gcm_out = gcm_out.reshape(FIELDS, 4, 2, 4, 4, LEVELS).transpose(0, 5, 1, 2, 3, 4)
    return cloud, gcm_out


def solution(mesh):
    return jax.shard_map(
        body,
        mesh=mesh,
        in_specs=(
            P(None, None, None, ("ex", "ey")),
            P(None, None, "ex", "ey", None, None),
            P(None, "ex", "ey", None, None),
            P(("ex", "ey"), None),
            P(("ex", "ey")),
        ),
        out_specs=(P(None, None, None, ("ex", "ey")), P(None, None, "ex", "ey", None, None)),
        check_vma=False,
    )
```

```python
import functools
import random

import jax
import jax.numpy as jnp
from jax import lax
from jax.experimental import pallas as pl
from jax.experimental.pallas import tpu as pltpu
from jax.sharding import PartitionSpec as P

MESH = pl.DeviceIdType.MESH
HIGHEST = lax.Precision.HIGHEST
FIELDS, LEVELS, WIDTH, OWNED, DEVICES = 5, 12, 32, 128, 128
N_EX, N_EY = 16, 8
HALO_ROWS = 80
BLOCKS = 6
BLOCK_ROWS = DEVICES * FIELDS
HALOS = (
    (0, 8, -1, 0),
    (8, 8, 1, 0),
    (16, 16, 0, -1),
    (32, 16, 0, 1),
    (48, 8, -1, -1),
    (56, 8, -1, 1),
    (64, 8, 1, -1),
    (72, 8, 1, 1),
)


def far_first():
    steps = [
        (dx, dy, dz, dc)
        for dx in range(4)
        for dy in range(4)
        for dz in range(4)
        for dc in range(2)
    ][1:]
    random.Random(0).shuffle(steps)
    return sorted(steps, key=lambda s: -sum(min(v, 4 - v) for v in s[:3]))


STEPS = far_first()
X_STEPS = [(d, 0, 0, 0) for d in (2, 1, 3)]
Y_STEPS = [(0, d, 0, 0) for d in (2, 1, 3)]
Z_STEPS = [(0, 0, d, 0) for d in (2, 1, 3)]
NEAR_STEPS = [s for s in STEPS if sum(v != 0 for v in s[:3]) < 2]
SIDE_STEPS = [s for s in STEPS if s not in NEAR_STEPS and 0 in s[:3]]
FAR_STEPS = [s for s in STEPS if 0 not in s[:3]]

CHIPS = [s[:3] for s in STEPS if s[3] == 0]
CORE_STEPS = [(*chip, None, core) for core in (1, 0) for chip in CHIPS] + [(0, 0, 0, 1)]


def nt_dot(a, b, precision=None):
    return lax.dot_general(
        a, b, (((1,), (1,)), ((), ())), precision=precision, preferred_element_type=jnp.float32
    )


def tn_dot(a, b, precision=None):
    return lax.dot_general(
        a, b, (((0,), (0,)), ((), ())), precision=precision, preferred_element_type=jnp.float32
    )


def level_step(source, z, profiles, means):
    values = [source[f, z + 1, 8:40] for f in range(FIELDS)]
    drift = 0.075 * values[0]
    condensed = 0.4 * jnp.maximum(values[3], 0.0)
    after = []
    for f in range(FIELDS):
        s = values[f]
        west, east = source[f, z + 1, 7:39], source[f, z + 1, 9:41]
        mean = jnp.sum(s, axis=0, keepdims=True) * (1.0 / WIDTH)
        if means is not None:
            means[pl.ds(f * LEVELS + z, 1), :] = mean
        nudged = 0.5 * (profiles[pl.ds(f * LEVELS + z, 1), :] - mean)
        near = (east + west) + (source[f, z + 2, 8:40] + source[f, z, 8:40])
        kept = 0.4 if f == 4 else 0.6
        new = (kept * s + 0.1 * near) - drift * (east - west) + nudged
        if f == 1:
            new = new + 0.3 * values[2]
        elif f == 2:
            new = new - 0.3 * values[1] + 0.5 * condensed
        elif f == 3:
            new = new - condensed
        elif f == 4:
            new = new + condensed
        after.append(new)
    return values, after


def cloud_kernel(
    crm, gcm_hbm, mass_hbm, dest_hbm, cost_hbm, landed, gcm_out,
    start, first, second, profiles, means, weighted, faces, halo, outgoing,
    gcm, gcm_new, mass, dest, cost, load_sem, stage_sem, own_sem, send_sem, recv_sem, face_send, face_recv,
):
    ex, ey = lax.axis_index("ex"), lax.axis_index("ey")
    me = ex * N_EY + ey
    px, pz, py, pc = ex // 4, ex % 4, ey // 2, ey % 2

    at_ex = [[((px + dx) % 4) * 4 + (pz + dz) % 4 for dz in range(4)] for dx in range(4)]
    at_ey = [[((py + dy) % 4) * 2 + (pc + dc) % 2 for dc in range(2)] for dy in range(4)]

    def peer(step):
        dx, dy, dz, dc, *core = step
        if core:
            return at_ex[dx][dz], (py + dy) % 4 * 2 + core[0]
        return at_ex[dx][dz], at_ey[dy][dc]

    loads = [
        pltpu.make_async_copy(source, into, load_sem.at[i])
        for i, (source, into) in enumerate(
            (
                (dest_hbm, dest),
                (gcm_hbm, gcm),
                (mass_hbm, mass),
                (cost_hbm, cost),
                (crm.at[:, pl.ds(0, 6)], start.at[:, pl.ds(1, 6), pl.ds(8, WIDTH)]),
                (crm.at[:, :, pl.ds(WIDTH - 1, 1)], start.at[:, pl.ds(1, LEVELS), pl.ds(7, 1)]),
                (crm.at[:, :, pl.ds(0, 1)], start.at[:, pl.ds(1, LEVELS), pl.ds(40, 1)]),
                (crm.at[:, pl.ds(6, 6)], start.at[:, pl.ds(7, 6), pl.ds(8, WIDTH)]),
            )
        )
    ]
    for load in loads:
        load.start()
    def signal(semaphore, steps):
        for step in steps:
            pl.semaphore_signal(semaphore, inc=1, device_id=peer(step), device_id_type=MESH)

    barrier = pltpu.get_barrier_semaphore()
    signal(barrier, NEAR_STEPS)

    loads[0].wait()
    row = lax.broadcasted_iota(jnp.int32, (OWNED, OWNED), 0)
    lane = lax.broadcasted_iota(jnp.int32, (OWNED, OWNED), 1)
    target = dest[...].astype(jnp.float32)
    target_rows = jnp.sum(jnp.where(row == lane, target, 0.0), axis=1, keepdims=True)
    earlier = jnp.where((target_rows == target) & (row < lane), 1.0, 0.0)
    slot = jnp.sum(earlier, axis=0, keepdims=True) * DEVICES + target
    slots = lax.broadcasted_iota(jnp.int32, (2 * DEVICES, OWNED), 0).astype(jnp.float32)
    chosen = jnp.where(slots == slot, 1.0, 0.0).astype(jnp.bfloat16)

    loads[1].wait()
    loads[2].wait()
    for f in range(FIELDS):
        profiles[f * LEVELS:(f + 1) * LEVELS, :] = jnp.swapaxes(gcm[f], 0, 1)
    mass_rows = jnp.swapaxes(mass[...], 0, 1)

    zero = jnp.zeros((WIDTH, OWNED), jnp.float32)
    for f in range(FIELDS):
        for z in (0, LEVELS + 1):
            start[f, z, 8:40] = zero
            first[f, z, 8:40] = zero
    for load in loads[3:7]:
        load.wait()
    twice = cost[...].astype(jnp.float32) >= 2.0

    chosen_pair = jnp.concatenate([chosen, chosen], axis=1)

    def advance_once(first_level, last_level):
        @pl.loop(first_level, last_level)
        def _(z):
            _, after = level_step(start, z, profiles, means)
            for f in range(FIELDS):
                first[f, z + 1, 8:40] = after[f]
                first[f, z + 1, 7:8] = after[f][WIDTH - 1:]
                first[f, z + 1, 40:41] = after[f][:1]

    def advance_twice(first_level, last_level):
        @pl.loop(first_level, last_level, unroll=2)
        def _(z):
            values, after = level_step(first, z, profiles, None)
            for f in range(FIELDS):
                updated = jnp.where(twice, after[f], values[f])
                second[f, z] = updated
                at = pl.ds(f * LEVELS + z, 1)
                mean = jnp.sum(updated, axis=0, keepdims=True) * (1.0 / WIDTH)
                weighted[at, :] = mean - means[at, :]

    def select(part):
        for f in range(FIELDS):
            block = second[f, 4 * part:4 * part + 4].reshape(128, OWNED)
            high = block.astype(jnp.bfloat16)
            low = (block - high.astype(jnp.float32)).astype(jnp.bfloat16)
            moved = nt_dot(chosen_pair, jnp.concatenate([high, low], axis=1))
            for r in range(2):
                outgoing[2 * part + r, pl.ds(f, DEVICES, stride=FIELDS), :] = moved[
                    r * DEVICES:(r + 1) * DEVICES
                ]

    def piece(buffer, group, device):
        blocks = pl.ds(2, 4) if group else pl.ds(0, 2)
        return buffer.at[blocks, pl.ds(device * FIELDS, FIELDS)]

    def send(part, steps):
        for step in steps:
            there_ex, there_ey = peer(step)
            pltpu.make_async_remote_copy(
                src_ref=piece(outgoing, part, there_ex * N_EY + there_ey),
                dst_ref=piece(landed, part, me),
                send_sem=send_sem,
                recv_sem=recv_sem,
                device_id=(there_ex, there_ey),
                device_id_type=MESH,
            ).start()

    pl.semaphore_wait(barrier, len(NEAR_STEPS))
    signal(stage_sem.at[0], X_STEPS + Y_STEPS + Z_STEPS)
    advance_once(0, 5)
    advance_twice(0, 4)
    select(0)
    send(0, NEAR_STEPS)
    pl.semaphore_wait(stage_sem.at[0], 9)
    signal(stage_sem.at[1], Y_STEPS)
    send(0, SIDE_STEPS)
    loads[7].wait()
    advance_once(5, 12)
    advance_twice(4, 12)
    select(1)
    select(2)
    pl.semaphore_wait(stage_sem.at[1], 3)
    send(0, FAR_STEPS)
    for f in range(FIELDS):
        rows = slice(f * LEVELS, (f + 1) * LEVELS)
        weighted[rows, :] = (weighted[rows, :] + profiles[rows, :]) * mass_rows
    weighted[60:72, :] = mass_rows
    weighted[72:128, :] = jnp.zeros((56, OWNED), jnp.float32)
    hrow = lax.broadcasted_iota(jnp.int32, (HALO_ROWS, OWNED), 0)
    hlane = lax.broadcasted_iota(jnp.int32, (HALO_ROWS, OWNED), 1)
    x_node = (hrow % 8 // 4) * 16 + hrow % 4
    y_node = ((hrow % 16) // 4) * 32 + (hrow % 4) * 4
    node = jnp.where(hrow < 8, x_node, x_node + 108)
    node = jnp.where(hrow < 16, node, jnp.where(hrow < 32, y_node, y_node + 19))
    corner = jnp.where(hrow == 48, 0, jnp.where(hrow == 56, 19, jnp.where(hrow == 64, 108, 127)))
    corner = jnp.where(hrow % 8 == 0, corner, -1)
    node = jnp.where(hrow < 48, node, corner)
    faces[...] = nt_dot(jnp.where(node == hlane, 1.0, 0.0), weighted[...], HIGHEST)

    face_copies = []
    for i, (at, rows, sx, sy) in enumerate(HALOS):
        copy = pltpu.make_async_remote_copy(
            src_ref=faces.at[pl.ds(at, rows)],
            dst_ref=halo.at[pl.ds(at, rows)],
            send_sem=face_send.at[i],
            recv_sem=face_recv.at[i],
            device_id=((ex + sx + N_EX) % N_EX, (ey + sy + N_EY) % N_EY),
            device_id_type=MESH,
        )
        copy.start()
        face_copies.append(copy)
    send(1, CORE_STEPS)
    owns = []
    for part in range(2):
        own = pltpu.make_async_copy(
            piece(outgoing, part, me), piece(landed, part, me), own_sem.at[part]
        )
        own.start()
        owns.append(own)

    def place(index):
        across = (index // 32) * 3 + index % 16 // 4
        along = (index // 16 % 2) * 3 + index % 4
        return across * 8 + along

    for copy in face_copies:
        copy.wait()
    shared = jnp.where(place(row) == place(lane), 1.0, 0.0)
    hside = jnp.where(hrow < 8, 96, 0) + (hrow % 8 // 4) * 3 + hrow % 4
    hfront = ((hrow % 16 // 4) * 3 + hrow % 4) * 8 + jnp.where(hrow < 32, 6, 0)
    hcorner = jnp.where(
        hrow == 48, 102, jnp.where(hrow == 56, 96, jnp.where(hrow == 64, 6, 0))
    )
    hcorner = jnp.where(hrow % 8 == 0, hcorner, -1)
    hplace = jnp.where(hrow < 16, hside, jnp.where(hrow < 48, hfront, hcorner))
    met = jnp.where(hplace == place(hlane), 1.0, 0.0)
    summed = jnp.dot(weighted[...], shared, precision=HIGHEST, preferred_element_type=jnp.float32)
    summed = summed + tn_dot(halo[...], met, HIGHEST)
    below = summed[60:72]
    for f in range(FIELDS):
        gcm_new[f] = jnp.swapaxes(summed[f * LEVELS:(f + 1) * LEVELS] / below, 0, 1)

    store = pltpu.make_async_copy(gcm_new, gcm_out, load_sem.at[0])
    store.start()
    for own in owns:
        own.wait()
    store.wait()
    others = pl.ds(0, (DEVICES - 1) * FIELDS)
    pltpu.make_async_copy(outgoing.at[:, others], outgoing.at[:, others], send_sem).wait()
    pltpu.make_async_copy(landed.at[:, others], landed.at[:, others], recv_sem).wait()


def unpack_kernel(landed, gcm_in, cloud, gcm_out, laid, out_sem):
    stores = [pltpu.make_async_copy(gcm_in, gcm_out, out_sem.at[15])]
    stores[0].start()
    for part in range(3):
        for f in range(FIELDS):
            rows = pl.ds(part * 128, 128)
            for r in range(2):
                lanes = pl.ds(r * DEVICES, DEVICES)
                laid[f, rows, lanes] = landed[2 * part + r, pl.ds(f, DEVICES, stride=FIELDS), :].T
            store = pltpu.make_async_copy(
                laid.at[f, rows], cloud.at[f, rows], out_sem.at[part * FIELDS + f]
            )
            store.start()
            stores.append(store)
    for store in stores:
        store.wait()


def body(crm_state, gcm_state, mass, dest, cost_class):
    any_space = pl.BlockSpec(memory_space=pl.ANY)
    gcm_rows = gcm_state.transpose(0, 2, 3, 4, 5, 1).reshape(FIELDS, OWNED, LEVELS)
    mass_rows = mass.transpose(1, 2, 3, 4, 0).reshape(OWNED, LEVELS)
    landed, gcm_out = pl.pallas_call(
        cloud_kernel,
        out_shape=(
            jax.ShapeDtypeStruct((BLOCKS, BLOCK_ROWS, 128), jnp.float32),
            jax.ShapeDtypeStruct((FIELDS, OWNED, LEVELS), jnp.float32),
        ),
        in_specs=[pl.BlockSpec(memory_space=pltpu.HBM)] * 5,
        out_specs=(any_space, any_space),
        scratch_shapes=[
            pltpu.VMEM((FIELDS, LEVELS + 2, 48, OWNED), jnp.float32),
            pltpu.VMEM((FIELDS, LEVELS + 2, 48, OWNED), jnp.float32),
            pltpu.VMEM((FIELDS, LEVELS, WIDTH, OWNED), jnp.float32),
            pltpu.VMEM((FIELDS * LEVELS, OWNED), jnp.float32),
            pltpu.VMEM((FIELDS * LEVELS, OWNED), jnp.float32),
            pltpu.VMEM((128, OWNED), jnp.float32),
            pltpu.VMEM((HALO_ROWS, 128), jnp.float32),
            pltpu.VMEM((HALO_ROWS, 128), jnp.float32),
            pltpu.VMEM((BLOCKS, BLOCK_ROWS, 128), jnp.float32),
            pltpu.VMEM((FIELDS, OWNED, LEVELS), jnp.float32),
            pltpu.VMEM((FIELDS, OWNED, LEVELS), jnp.float32),
            pltpu.VMEM((OWNED, LEVELS), jnp.float32),
            pltpu.VMEM((1, OWNED), jnp.int32),
            pltpu.VMEM((1, OWNED), jnp.int32),
            pltpu.SemaphoreType.DMA((8,)),
            pltpu.SemaphoreType.REGULAR((2,)),
            pltpu.SemaphoreType.DMA((3,)),
            pltpu.SemaphoreType.DMA,
            pltpu.SemaphoreType.DMA,
            pltpu.SemaphoreType.DMA((8,)),
            pltpu.SemaphoreType.DMA((8,)),
        ],
        compiler_params=pltpu.CompilerParams(
            collective_id=0, has_side_effects=True, vmem_limit_bytes=40 * 2**20
        ),
        name="clouds",
    )(*(pltpu.with_memory_space_constraint(v, pltpu.HBM) for v in (crm_state, gcm_rows, mass_rows, dest.reshape(1, OWNED), cost_class.reshape(1, OWNED))))
    cloud, gcm_out = pl.pallas_call(
        unpack_kernel,
        out_shape=(
            jax.ShapeDtypeStruct((FIELDS, LEVELS * WIDTH, 2 * DEVICES), jnp.float32),
            jax.ShapeDtypeStruct((FIELDS, OWNED, LEVELS), jnp.float32),
        ),
        in_specs=[pl.BlockSpec(memory_space=pltpu.VMEM), pl.BlockSpec(memory_space=pltpu.VMEM)],
        out_specs=(any_space, any_space),
        scratch_shapes=[
            pltpu.VMEM((FIELDS, LEVELS * WIDTH, 2 * DEVICES), jnp.float32),
            pltpu.SemaphoreType.DMA((16,)),
        ],
        compiler_params=pltpu.CompilerParams(vmem_limit_bytes=16 * 2**20),
        name="unpack",
    )(landed, gcm_out)
    cloud = cloud.reshape(FIELDS, LEVELS, WIDTH, 2 * DEVICES)
    gcm_out = gcm_out.reshape(FIELDS, 4, 2, 4, 4, LEVELS).transpose(0, 5, 1, 2, 3, 4)
    return cloud, gcm_out


def solution(mesh):
    return jax.shard_map(
        body,
        mesh=mesh,
        in_specs=(
            P(None, None, None, ("ex", "ey")),
            P(None, None, "ex", "ey", None, None),
            P(None, "ex", "ey", None, None),
            P(("ex", "ey"), None),
            P(("ex", "ey")),
        ),
        out_specs=(P(None, None, None, ("ex", "ey")), P(None, None, "ex", "ey", None, None)),
        check_vma=False,
    )
```

```python
import functools
import random

import jax
import jax.numpy as jnp
from jax import lax
from jax.experimental import pallas as pl
from jax.experimental.pallas import tpu as pltpu
from jax.sharding import PartitionSpec as P

MESH = pl.DeviceIdType.MESH
HIGHEST = lax.Precision.HIGHEST
FIELDS, LEVELS, WIDTH, OWNED, DEVICES = 5, 12, 32, 128, 128
N_EX, N_EY = 16, 8
HALO_ROWS = 80
BLOCKS = 6
BLOCK_ROWS = DEVICES * FIELDS
HALOS = (
    (0, 8, -1, 0),
    (8, 8, 1, 0),
    (16, 16, 0, -1),
    (32, 16, 0, 1),
    (48, 8, -1, -1),
    (56, 8, -1, 1),
    (64, 8, 1, -1),
    (72, 8, 1, 1),
)


def far_first():
    steps = [
        (dx, dy, dz, dc)
        for dx in range(4)
        for dy in range(4)
        for dz in range(4)
        for dc in range(2)
    ][1:]
    random.Random(0).shuffle(steps)
    return sorted(steps, key=lambda s: -sum(min(v, 4 - v) for v in s[:3]))


STEPS = far_first()
X_STEPS = [(d, 0, 0, 0) for d in (2, 1, 3)]
Y_STEPS = [(0, d, 0, 0) for d in (2, 1, 3)]
Z_STEPS = [(0, 0, d, 0) for d in (2, 1, 3)]
NEAR_STEPS = [s for s in STEPS if sum(v != 0 for v in s[:3]) < 2]
SIDE_STEPS = [s for s in STEPS if s not in NEAR_STEPS and 0 in s[:3]]
FAR_STEPS = [s for s in STEPS if 0 not in s[:3]]

CHIPS = [s[:3] for s in STEPS if s[3] == 0]
CORE_STEPS = [
    (*chip, None, core)
    for chips in (CHIPS[:32], CHIPS[32:])
    for core in (1, 0)
    for chip in chips
] + [(0, 0, 0, 1)]


def nt_dot(a, b, precision=None):
    return lax.dot_general(
        a, b, (((1,), (1,)), ((), ())), precision=precision, preferred_element_type=jnp.float32
    )


def tn_dot(a, b, precision=None):
    return lax.dot_general(
        a, b, (((0,), (0,)), ((), ())), precision=precision, preferred_element_type=jnp.float32
    )


def level_step(source, z, profiles, means):
    values = [source[f, z + 1, 8:40] for f in range(FIELDS)]
    drift = 0.075 * values[0]
    condensed = 0.4 * jnp.maximum(values[3], 0.0)
    after = []
    for f in range(FIELDS):
        s = values[f]
        west, east = source[f, z + 1, 7:39], source[f, z + 1, 9:41]
        mean = jnp.sum(s, axis=0, keepdims=True) * (1.0 / WIDTH)
        if means is not None:
            means[pl.ds(f * LEVELS + z, 1), :] = mean
        nudged = 0.5 * (profiles[pl.ds(f * LEVELS + z, 1), :] - mean)
        near = (east + west) + (source[f, z + 2, 8:40] + source[f, z, 8:40])
        kept = 0.4 if f == 4 else 0.6
        new = (kept * s + 0.1 * near) - drift * (east - west) + nudged
        if f == 1:
            new = new + 0.3 * values[2]
        elif f == 2:
            new = new - 0.3 * values[1] + 0.5 * condensed
        elif f == 3:
            new = new - condensed
        elif f == 4:
            new = new + condensed
        after.append(new)
    return values, after


def cloud_kernel(
    crm, gcm_hbm, mass_hbm, dest_hbm, cost_hbm, landed, gcm_out,
    start, first, second, profiles, means, weighted, faces, halo, outgoing,
    gcm, gcm_new, mass, dest, cost, load_sem, stage_sem, own_sem, send_sem, recv_sem, face_send, face_recv,
):
    ex, ey = lax.axis_index("ex"), lax.axis_index("ey")
    me = ex * N_EY + ey
    px, pz, py, pc = ex // 4, ex % 4, ey // 2, ey % 2

    at_ex = [[((px + dx) % 4) * 4 + (pz + dz) % 4 for dz in range(4)] for dx in range(4)]
    at_ey = [[((py + dy) % 4) * 2 + (pc + dc) % 2 for dc in range(2)] for dy in range(4)]

    def peer(step):
        dx, dy, dz, dc, *core = step
        if core:
            return at_ex[dx][dz], (py + dy) % 4 * 2 + core[0]
        return at_ex[dx][dz], at_ey[dy][dc]

    loads = [
        pltpu.make_async_copy(source, into, load_sem.at[i])
        for i, (source, into) in enumerate(
            (
                (dest_hbm, dest),
                (gcm_hbm, gcm),
                (mass_hbm, mass),
                (cost_hbm, cost),
                (crm.at[:, pl.ds(0, 6)], start.at[:, pl.ds(1, 6), pl.ds(8, WIDTH)]),
                (crm.at[:, :, pl.ds(WIDTH - 1, 1)], start.at[:, pl.ds(1, LEVELS), pl.ds(7, 1)]),
                (crm.at[:, :, pl.ds(0, 1)], start.at[:, pl.ds(1, LEVELS), pl.ds(40, 1)]),
                (crm.at[:, pl.ds(6, 6)], start.at[:, pl.ds(7, 6), pl.ds(8, WIDTH)]),
            )
        )
    ]
    for load in loads:
        load.start()
    def signal(semaphore, steps):
        for step in steps:
            pl.semaphore_signal(semaphore, inc=1, device_id=peer(step), device_id_type=MESH)

    barrier = pltpu.get_barrier_semaphore()
    signal(barrier, NEAR_STEPS)

    loads[0].wait()
    row = lax.broadcasted_iota(jnp.int32, (OWNED, OWNED), 0)
    lane = lax.broadcasted_iota(jnp.int32, (OWNED, OWNED), 1)
    target = dest[...].astype(jnp.float32)
    target_rows = jnp.sum(jnp.where(row == lane, target, 0.0), axis=1, keepdims=True)
    earlier = jnp.where((target_rows == target) & (row < lane), 1.0, 0.0)
    slot = jnp.sum(earlier, axis=0, keepdims=True) * DEVICES + target
    slots = lax.broadcasted_iota(jnp.int32, (2 * DEVICES, OWNED), 0).astype(jnp.float32)
    chosen = jnp.where(slots == slot, 1.0, 0.0).astype(jnp.bfloat16)

    loads[1].wait()
    loads[2].wait()
    for f in range(FIELDS):
        profiles[f * LEVELS:(f + 1) * LEVELS, :] = jnp.swapaxes(gcm[f], 0, 1)
    mass_rows = jnp.swapaxes(mass[...], 0, 1)

    zero = jnp.zeros((WIDTH, OWNED), jnp.float32)
    for f in range(FIELDS):
        for z in (0, LEVELS + 1):
            start[f, z, 8:40] = zero
            first[f, z, 8:40] = zero
    for load in loads[3:7]:
        load.wait()
    twice = cost[...].astype(jnp.float32) >= 2.0

    chosen_pair = jnp.concatenate([chosen, chosen], axis=1)

    def advance_once(first_level, last_level):
        @pl.loop(first_level, last_level)
        def _(z):
            _, after = level_step(start, z, profiles, means)
            for f in range(FIELDS):
                first[f, z + 1, 8:40] = after[f]
                first[f, z + 1, 7:8] = after[f][WIDTH - 1:]
                first[f, z + 1, 40:41] = after[f][:1]

    def advance_twice(first_level, last_level):
        @pl.loop(first_level, last_level, unroll=2)
        def _(z):
            values, after = level_step(first, z, profiles, None)
            for f in range(FIELDS):
                updated = jnp.where(twice, after[f], values[f])
                second[f, z] = updated
                at = pl.ds(f * LEVELS + z, 1)
                mean = jnp.sum(updated, axis=0, keepdims=True) * (1.0 / WIDTH)
                weighted[at, :] = mean - means[at, :]

    def select(part):
        for f in range(FIELDS):
            block = second[f, 4 * part:4 * part + 4].reshape(128, OWNED)
            high = block.astype(jnp.bfloat16)
            low = (block - high.astype(jnp.float32)).astype(jnp.bfloat16)
            moved = nt_dot(chosen_pair, jnp.concatenate([high, low], axis=1))
            for r in range(2):
                outgoing[2 * part + r, pl.ds(f, DEVICES, stride=FIELDS), :] = moved[
                    r * DEVICES:(r + 1) * DEVICES
                ]

    def piece(buffer, group, device):
        blocks = pl.ds(2, 4) if group else pl.ds(0, 2)
        return buffer.at[blocks, pl.ds(device * FIELDS, FIELDS)]

    def send(part, steps):
        for step in steps:
            there_ex, there_ey = peer(step)
            pltpu.make_async_remote_copy(
                src_ref=piece(outgoing, part, there_ex * N_EY + there_ey),
                dst_ref=piece(landed, part, me),
                send_sem=send_sem,
                recv_sem=recv_sem,
                device_id=(there_ex, there_ey),
                device_id_type=MESH,
            ).start()

    pl.semaphore_wait(barrier, len(NEAR_STEPS))
    signal(stage_sem.at[0], X_STEPS + Y_STEPS + Z_STEPS)
    advance_once(0, 5)
    advance_twice(0, 4)
    select(0)
    send(0, NEAR_STEPS)
    pl.semaphore_wait(stage_sem.at[0], 9)
    signal(stage_sem.at[1], Y_STEPS)
    send(0, SIDE_STEPS)
    loads[7].wait()
    advance_once(5, 12)
    advance_twice(4, 12)
    select(1)
    select(2)
    pl.semaphore_wait(stage_sem.at[1], 3)
    send(0, FAR_STEPS)
    for f in range(FIELDS):
        rows = slice(f * LEVELS, (f + 1) * LEVELS)
        weighted[rows, :] = (weighted[rows, :] + profiles[rows, :]) * mass_rows
    weighted[60:72, :] = mass_rows
    weighted[72:128, :] = jnp.zeros((56, OWNED), jnp.float32)
    hrow = lax.broadcasted_iota(jnp.int32, (HALO_ROWS, OWNED), 0)
    hlane = lax.broadcasted_iota(jnp.int32, (HALO_ROWS, OWNED), 1)
    x_node = (hrow % 8 // 4) * 16 + hrow % 4
    y_node = ((hrow % 16) // 4) * 32 + (hrow % 4) * 4
    node = jnp.where(hrow < 8, x_node, x_node + 108)
    node = jnp.where(hrow < 16, node, jnp.where(hrow < 32, y_node, y_node + 19))
    corner = jnp.where(hrow == 48, 0, jnp.where(hrow == 56, 19, jnp.where(hrow == 64, 108, 127)))
    corner = jnp.where(hrow % 8 == 0, corner, -1)
    node = jnp.where(hrow < 48, node, corner)
    faces[...] = nt_dot(jnp.where(node == hlane, 1.0, 0.0), weighted[...], HIGHEST)

    for i, (at, rows, sx, sy) in enumerate(HALOS):
        copy = pltpu.make_async_remote_copy(
            src_ref=faces.at[pl.ds(at, rows)],
            dst_ref=halo.at[pl.ds(at, rows)],
            send_sem=face_send,
            recv_sem=face_recv,
            device_id=((ex + sx + N_EX) % N_EX, (ey + sy + N_EY) % N_EY),
            device_id_type=MESH,
        )
        copy.start()
    send(1, CORE_STEPS)
    mine = pl.ds(me * FIELDS, FIELDS)
    own = pltpu.make_async_copy(outgoing.at[:, mine], landed.at[:, mine], own_sem)
    own.start()

    def place(index):
        across = (index // 32) * 3 + index % 16 // 4
        along = (index // 16 % 2) * 3 + index % 4
        return across * 8 + along

    pltpu.make_async_copy(faces, faces, face_send).wait()
    pltpu.make_async_copy(halo, halo, face_recv).wait()
    shared = jnp.where(place(row) == place(lane), 1.0, 0.0)
    hside = jnp.where(hrow < 8, 96, 0) + (hrow % 8 // 4) * 3 + hrow % 4
    hfront = ((hrow % 16 // 4) * 3 + hrow % 4) * 8 + jnp.where(hrow < 32, 6, 0)
    hcorner = jnp.where(
        hrow == 48, 102, jnp.where(hrow == 56, 96, jnp.where(hrow == 64, 6, 0))
    )
    hcorner = jnp.where(hrow % 8 == 0, hcorner, -1)
    hplace = jnp.where(hrow < 16, hside, jnp.where(hrow < 48, hfront, hcorner))
    met = jnp.where(hplace == place(hlane), 1.0, 0.0)
    summed = jnp.dot(weighted[...], shared, precision=HIGHEST, preferred_element_type=jnp.float32)
    summed = summed + tn_dot(halo[...], met, HIGHEST)
    below = summed[60:72]
    for f in range(FIELDS):
        gcm_new[f] = jnp.swapaxes(summed[f * LEVELS:(f + 1) * LEVELS] / below, 0, 1)

    store = pltpu.make_async_copy(gcm_new, gcm_out, load_sem.at[0])
    store.start()
    own.wait()
    store.wait()
    others = pl.ds(0, (DEVICES - 1) * FIELDS)
    pltpu.make_async_copy(outgoing.at[:, others], outgoing.at[:, others], send_sem).wait()
    pltpu.make_async_copy(landed.at[:, others], landed.at[:, others], recv_sem).wait()


def unpack_kernel(landed, gcm_in, cloud, gcm_out, laid, gcm_sem, out_sem):
    gcm_store = pltpu.make_async_copy(gcm_in, gcm_out, gcm_sem)
    gcm_store.start()
    for part in range(3):
        for f in range(FIELDS):
            rows = pl.ds(part * 128, 128)
            for r in range(2):
                lanes = pl.ds(r * DEVICES, DEVICES)
                laid[f, rows, lanes] = landed[2 * part + r, pl.ds(f, DEVICES, stride=FIELDS), :].T
            pltpu.make_async_copy(laid.at[f, rows], cloud.at[f, rows], out_sem).start()
    gcm_store.wait()
    pltpu.make_async_copy(laid, cloud, out_sem).wait()


def body(crm_state, gcm_state, mass, dest, cost_class):
    any_space = pl.BlockSpec(memory_space=pl.ANY)
    gcm_rows = gcm_state.transpose(0, 2, 3, 4, 5, 1).reshape(FIELDS, OWNED, LEVELS)
    mass_rows = mass.transpose(1, 2, 3, 4, 0).reshape(OWNED, LEVELS)
    landed, gcm_out = pl.pallas_call(
        cloud_kernel,
        out_shape=(
            jax.ShapeDtypeStruct((BLOCKS, BLOCK_ROWS, 128), jnp.float32),
            jax.ShapeDtypeStruct((FIELDS, OWNED, LEVELS), jnp.float32),
        ),
        in_specs=[pl.BlockSpec(memory_space=pltpu.HBM)] * 5,
        out_specs=(any_space, any_space),
        scratch_shapes=[
            pltpu.VMEM((FIELDS, LEVELS + 2, 48, OWNED), jnp.float32),
            pltpu.VMEM((FIELDS, LEVELS + 2, 48, OWNED), jnp.float32),
            pltpu.VMEM((FIELDS, LEVELS, WIDTH, OWNED), jnp.float32),
            pltpu.VMEM((FIELDS * LEVELS, OWNED), jnp.float32),
            pltpu.VMEM((FIELDS * LEVELS, OWNED), jnp.float32),
            pltpu.VMEM((128, OWNED), jnp.float32),
            pltpu.VMEM((HALO_ROWS, 128), jnp.float32),
            pltpu.VMEM((HALO_ROWS, 128), jnp.float32),
            pltpu.VMEM((BLOCKS, BLOCK_ROWS, 128), jnp.float32),
            pltpu.VMEM((FIELDS, OWNED, LEVELS), jnp.float32),
            pltpu.VMEM((FIELDS, OWNED, LEVELS), jnp.float32),
            pltpu.VMEM((OWNED, LEVELS), jnp.float32),
            pltpu.VMEM((1, OWNED), jnp.int32),
            pltpu.VMEM((1, OWNED), jnp.int32),
            pltpu.SemaphoreType.DMA((8,)),
            pltpu.SemaphoreType.REGULAR((2,)),
            pltpu.SemaphoreType.DMA,
            pltpu.SemaphoreType.DMA,
            pltpu.SemaphoreType.DMA,
            pltpu.SemaphoreType.DMA,
            pltpu.SemaphoreType.DMA,
        ],
        compiler_params=pltpu.CompilerParams(
            collective_id=0, has_side_effects=True, vmem_limit_bytes=40 * 2**20
        ),
        name="clouds",
    )(*(pltpu.with_memory_space_constraint(v, pltpu.HBM) for v in (crm_state, gcm_rows, mass_rows, dest.reshape(1, OWNED), cost_class.reshape(1, OWNED))))
    cloud, gcm_out = pl.pallas_call(
        unpack_kernel,
        out_shape=(
            jax.ShapeDtypeStruct((FIELDS, LEVELS * WIDTH, 2 * DEVICES), jnp.float32),
            jax.ShapeDtypeStruct((FIELDS, OWNED, LEVELS), jnp.float32),
        ),
        in_specs=[pl.BlockSpec(memory_space=pltpu.VMEM), pl.BlockSpec(memory_space=pltpu.VMEM)],
        out_specs=(any_space, any_space),
        scratch_shapes=[
            pltpu.VMEM((FIELDS, LEVELS * WIDTH, 2 * DEVICES), jnp.float32),
            pltpu.SemaphoreType.DMA,
            pltpu.SemaphoreType.DMA,
        ],
        compiler_params=pltpu.CompilerParams(vmem_limit_bytes=16 * 2**20),
        name="unpack",
    )(landed, gcm_out)
    cloud = cloud.reshape(FIELDS, LEVELS, WIDTH, 2 * DEVICES)
    gcm_out = gcm_out.reshape(FIELDS, 4, 2, 4, 4, LEVELS).transpose(0, 5, 1, 2, 3, 4)
    return cloud, gcm_out


def solution(mesh):
    return jax.shard_map(
        body,
        mesh=mesh,
        in_specs=(
            P(None, None, None, ("ex", "ey")),
            P(None, None, "ex", "ey", None, None),
            P(None, "ex", "ey", None, None),
            P(("ex", "ey"), None),
            P(("ex", "ey")),
        ),
        out_specs=(P(None, None, None, ("ex", "ey")), P(None, None, "ex", "ey", None, None)),
        check_vma=False,
    )
```

```python
import functools
import random

import jax
import jax.numpy as jnp
from jax import lax
from jax.experimental import pallas as pl
from jax.experimental.pallas import tpu as pltpu
from jax.sharding import PartitionSpec as P

MESH = pl.DeviceIdType.MESH
HIGHEST = lax.Precision.HIGHEST
FIELDS, LEVELS, WIDTH, OWNED, DEVICES = 5, 12, 32, 128, 128
N_EX, N_EY = 16, 8
HALO_ROWS = 80
BLOCKS = 6
SEMAPHORE_OF = (0, 1, 2, 3, 4, 4, 4, 5)
BLOCK_ROWS = DEVICES * FIELDS
HALOS = (
    (0, 8, -1, 0),
    (8, 8, 1, 0),
    (16, 16, 0, -1),
    (32, 16, 0, 1),
    (48, 1, -1, -1),
    (56, 1, -1, 1),
    (64, 1, 1, -1),
    (72, 1, 1, 1),
)


def far_first():
    steps = [
        (dx, dy, dz, dc)
        for dx in range(4)
        for dy in range(4)
        for dz in range(4)
        for dc in range(2)
    ][1:]
    random.Random(0).shuffle(steps)
    return sorted(steps, key=lambda s: -sum(min(v, 4 - v) for v in s[:3]))


STEPS = far_first()
X_STEPS = [(d, 0, 0, 0) for d in (2, 1, 3)]
Y_STEPS = [(0, d, 0, 0) for d in (2, 1, 3)]
Z_STEPS = [(0, 0, d, 0) for d in (2, 1, 3)]
NEAR_STEPS = [s for s in STEPS if sum(v != 0 for v in s[:3]) < 2]
SIDE_STEPS = [s for s in STEPS if s not in NEAR_STEPS and 0 in s[:3]]
FAR_STEPS = [s for s in STEPS if 0 not in s[:3]]

CHIPS = [s[:3] for s in STEPS if s[3] == 0]
CORE_STEPS = [
    (*chip, None, core)
    for chips in (CHIPS[:32], CHIPS[32:])
    for core in (1, 0)
    for chip in chips
] + [(0, 0, 0, 1)]


def nt_dot(a, b, precision=None):
    return lax.dot_general(
        a, b, (((1,), (1,)), ((), ())), precision=precision, preferred_element_type=jnp.float32
    )


def tn_dot(a, b, precision=None):
    return lax.dot_general(
        a, b, (((0,), (0,)), ((), ())), precision=precision, preferred_element_type=jnp.float32
    )


def level_step(source, z, profiles, means):
    values = [source[f, z + 1, 8:40] for f in range(FIELDS)]
    drift = 0.075 * values[0]
    condensed = 0.4 * jnp.maximum(values[3], 0.0)
    after = []
    for f in range(FIELDS):
        s = values[f]
        west, east = source[f, z + 1, 7:39], source[f, z + 1, 9:41]
        mean = jnp.sum(s, axis=0, keepdims=True) * (1.0 / WIDTH)
        if means is not None:
            means[pl.ds(f * LEVELS + z, 1), :] = mean
        nudged = 0.5 * (profiles[pl.ds(f * LEVELS + z, 1), :] - mean)
        near = (east + west) + (source[f, z + 2, 8:40] + source[f, z, 8:40])
        kept = 0.4 if f == 4 else 0.6
        new = (kept * s + 0.1 * near) - drift * (east - west) + nudged
        if f == 1:
            new = new + 0.3 * values[2]
        elif f == 2:
            new = new - 0.3 * values[1] + 0.5 * condensed
        elif f == 3:
            new = new - condensed
        elif f == 4:
            new = new + condensed
        after.append(new)
    return values, after


def cloud_kernel(
    crm, gcm_hbm, mass_hbm, dest_hbm, cost_hbm, landed, gcm_out,
    start, first, second, profiles, means, weighted, faces, halo, outgoing,
    gcm, gcm_new, mass, dest, cost, load_sem, stage_sem, own_sem, send_sem, recv_sem, face_send, face_recv,
):
    ex, ey = lax.axis_index("ex"), lax.axis_index("ey")
    me = ex * N_EY + ey
    px, pz, py, pc = ex // 4, ex % 4, ey // 2, ey % 2

    at_ex = [[((px + dx) % 4) * 4 + (pz + dz) % 4 for dz in range(4)] for dx in range(4)]
    at_ey = [[((py + dy) % 4) * 2 + (pc + dc) % 2 for dc in range(2)] for dy in range(4)]

    def peer(step):
        dx, dy, dz, dc, *core = step
        if core:
            return at_ex[dx][dz], (py + dy) % 4 * 2 + core[0]
        return at_ex[dx][dz], at_ey[dy][dc]

    loads = [
        pltpu.make_async_copy(source, into, load_sem.at[SEMAPHORE_OF[i]])
        for i, (source, into) in enumerate(
            (
                (dest_hbm, dest),
                (gcm_hbm, gcm),
                (mass_hbm, mass),
                (cost_hbm, cost),
                (crm.at[:, pl.ds(0, 6)], start.at[:, pl.ds(1, 6), pl.ds(8, WIDTH)]),
                (crm.at[:, :, pl.ds(WIDTH - 1, 1)], start.at[:, pl.ds(1, LEVELS), pl.ds(7, 1)]),
                (crm.at[:, :, pl.ds(0, 1)], start.at[:, pl.ds(1, LEVELS), pl.ds(40, 1)]),
                (crm.at[:, pl.ds(6, 6)], start.at[:, pl.ds(7, 6), pl.ds(8, WIDTH)]),
            )
        )
    ]
    for load in loads:
        load.start()
    def signal(semaphore, steps):
        for step in steps:
            pl.semaphore_signal(semaphore, inc=1, device_id=peer(step), device_id_type=MESH)

    barrier = pltpu.get_barrier_semaphore()
    signal(barrier, NEAR_STEPS)

    loads[0].wait()
    row = lax.broadcasted_iota(jnp.int32, (OWNED, OWNED), 0)
    lane = lax.broadcasted_iota(jnp.int32, (OWNED, OWNED), 1)
    target = dest[...].astype(jnp.float32)
    target_rows = jnp.sum(jnp.where(row == lane, target, 0.0), axis=1, keepdims=True)
    earlier = jnp.where((target_rows == target) & (row < lane), 1.0, 0.0)
    slot = jnp.sum(earlier, axis=0, keepdims=True) * DEVICES + target
    slots = lax.broadcasted_iota(jnp.int32, (2 * DEVICES, OWNED), 0).astype(jnp.float32)
    chosen = jnp.where(slots == slot, 1.0, 0.0).astype(jnp.bfloat16)

    loads[1].wait()
    loads[2].wait()
    for f in range(FIELDS):
        profiles[f * LEVELS:(f + 1) * LEVELS, :] = jnp.swapaxes(gcm[f], 0, 1)
    mass_rows = jnp.swapaxes(mass[...], 0, 1)

    zero = jnp.zeros((WIDTH, OWNED), jnp.float32)
    for f in range(FIELDS):
        for z in (0, LEVELS + 1):
            start[f, z, 8:40] = zero
            first[f, z, 8:40] = zero
    loads[3].wait()
    upper = outgoing.at[pl.ds(0, 3), pl.ds(0, 360)]
    pltpu.make_async_copy(upper, upper, load_sem.at[4]).wait()
    twice = cost[...].astype(jnp.float32) >= 2.0

    chosen_pair = jnp.concatenate([chosen, chosen], axis=1)

    def advance_once(first_level, last_level):
        @pl.loop(first_level, last_level)
        def _(z):
            _, after = level_step(start, z, profiles, means)
            for f in range(FIELDS):
                first[f, z + 1, 8:40] = after[f]
                first[f, z + 1, 7:8] = after[f][WIDTH - 1:]
                first[f, z + 1, 40:41] = after[f][:1]

    def advance_twice(first_level, last_level):
        @pl.loop(first_level, last_level, unroll=2)
        def _(z):
            values, after = level_step(first, z, profiles, None)
            for f in range(FIELDS):
                updated = jnp.where(twice, after[f], values[f])
                second[f, z] = updated
                at = pl.ds(f * LEVELS + z, 1)
                mean = jnp.sum(updated, axis=0, keepdims=True) * (1.0 / WIDTH)
                weighted[at, :] = mean - means[at, :]

    def select(part):
        for f in range(FIELDS):
            block = second[f, 4 * part:4 * part + 4].reshape(128, OWNED)
            high = block.astype(jnp.bfloat16)
            low = (block - high.astype(jnp.float32)).astype(jnp.bfloat16)
            moved = nt_dot(chosen_pair, jnp.concatenate([high, low], axis=1))
            for r in range(2):
                outgoing[2 * part + r, pl.ds(f, DEVICES, stride=FIELDS), :] = moved[
                    r * DEVICES:(r + 1) * DEVICES
                ]

    def piece(buffer, group, device):
        blocks = pl.ds(2, 4) if group else pl.ds(0, 2)
        return buffer.at[blocks, pl.ds(device * FIELDS, FIELDS)]

    def send(part, steps):
        for step in steps:
            there_ex, there_ey = peer(step)
            pltpu.make_async_remote_copy(
                src_ref=piece(outgoing, part, there_ex * N_EY + there_ey),
                dst_ref=piece(landed, part, me),
                send_sem=send_sem,
                recv_sem=recv_sem,
                device_id=(there_ex, there_ey),
                device_id_type=MESH,
            ).start()

    pl.semaphore_wait(barrier, len(NEAR_STEPS))
    signal(stage_sem.at[0], X_STEPS + Y_STEPS + Z_STEPS)
    advance_once(0, 5)
    advance_twice(0, 4)
    select(0)
    send(0, NEAR_STEPS)
    pl.semaphore_wait(stage_sem.at[0], 9)
    signal(stage_sem.at[1], Y_STEPS)
    send(0, SIDE_STEPS)
    loads[7].wait()
    advance_once(5, 12)
    advance_twice(4, 12)
    select(1)
    select(2)
    pl.semaphore_wait(stage_sem.at[1], 3)
    send(0, FAR_STEPS)
    for f in range(FIELDS):
        rows = slice(f * LEVELS, (f + 1) * LEVELS)
        weighted[rows, :] = (weighted[rows, :] + profiles[rows, :]) * mass_rows
    weighted[60:72, :] = mass_rows
    weighted[72:128, :] = jnp.zeros((56, OWNED), jnp.float32)
    hrow = lax.broadcasted_iota(jnp.int32, (HALO_ROWS, OWNED), 0)
    hlane = lax.broadcasted_iota(jnp.int32, (HALO_ROWS, OWNED), 1)
    x_node = (hrow % 8 // 4) * 16 + hrow % 4
    y_node = ((hrow % 16) // 4) * 32 + (hrow % 4) * 4
    node = jnp.where(hrow < 8, x_node, x_node + 108)
    node = jnp.where(hrow < 16, node, jnp.where(hrow < 32, y_node, y_node + 19))
    corner = jnp.where(hrow == 48, 0, jnp.where(hrow == 56, 19, jnp.where(hrow == 64, 108, 127)))
    corner = jnp.where(hrow % 8 == 0, corner, -1)
    node = jnp.where(hrow < 48, node, corner)
    faces[...] = nt_dot(jnp.where(node == hlane, 1.0, 0.0), weighted[...], HIGHEST)

    for i, (at, rows, sx, sy) in enumerate(HALOS):
        copy = pltpu.make_async_remote_copy(
            src_ref=faces.at[pl.ds(at, rows)],
            dst_ref=halo.at[pl.ds(at, rows)],
            send_sem=face_send,
            recv_sem=face_recv,
            device_id=((ex + sx + N_EX) % N_EX, (ey + sy + N_EY) % N_EY),
            device_id_type=MESH,
        )
        copy.start()
    send(1, CORE_STEPS)
    mine = pl.ds(me * FIELDS, FIELDS)
    own = pltpu.make_async_copy(outgoing.at[:, mine], landed.at[:, mine], own_sem)
    own.start()

    def place(index):
        across = (index // 32) * 3 + index % 16 // 4
        along = (index // 16 % 2) * 3 + index % 4
        return across * 8 + along

    moved_rows = pl.ds(0, 52)
    pltpu.make_async_copy(faces.at[moved_rows], faces.at[moved_rows], face_send).wait()
    pltpu.make_async_copy(halo.at[moved_rows], halo.at[moved_rows], face_recv).wait()
    shared = jnp.where(place(row) == place(lane), 1.0, 0.0)
    hside = jnp.where(hrow < 8, 96, 0) + (hrow % 8 // 4) * 3 + hrow % 4
    hfront = ((hrow % 16 // 4) * 3 + hrow % 4) * 8 + jnp.where(hrow < 32, 6, 0)
    hcorner = jnp.where(
        hrow == 48, 102, jnp.where(hrow == 56, 96, jnp.where(hrow == 64, 6, 0))
    )
    hcorner = jnp.where(hrow % 8 == 0, hcorner, -1)
    hplace = jnp.where(hrow < 16, hside, jnp.where(hrow < 48, hfront, hcorner))
    met = jnp.where(hplace == place(hlane), 1.0, 0.0)
    summed = jnp.dot(weighted[...], shared, precision=HIGHEST, preferred_element_type=jnp.float32)
    arrived = jnp.where((hrow < 48) | (hrow % 8 == 0), halo[...], 0.0)
    summed = summed + tn_dot(arrived, met, HIGHEST)
    below = summed[60:72]
    for f in range(FIELDS):
        gcm_new[f] = jnp.swapaxes(summed[f * LEVELS:(f + 1) * LEVELS] / below, 0, 1)

    store = pltpu.make_async_copy(gcm_new, gcm_out, load_sem.at[0])
    store.start()
    own.wait()
    store.wait()
    others = pl.ds(0, (DEVICES - 1) * FIELDS)
    pltpu.make_async_copy(outgoing.at[:, others], outgoing.at[:, others], send_sem).wait()
    pltpu.make_async_copy(landed.at[:, others], landed.at[:, others], recv_sem).wait()


def unpack_kernel(landed, gcm_in, cloud, gcm_out, laid, gcm_sem, out_sem):
    gcm_store = pltpu.make_async_copy(gcm_in, gcm_out, gcm_sem)
    gcm_store.start()
    for part in range(3):
        for f in range(FIELDS):
            rows = pl.ds(part * 128, 128)
            for r in range(2):
                lanes = pl.ds(r * DEVICES, DEVICES)
                laid[f, rows, lanes] = landed[2 * part + r, pl.ds(f, DEVICES, stride=FIELDS), :].T
            pltpu.make_async_copy(laid.at[f, rows], cloud.at[f, rows], out_sem).start()
    gcm_store.wait()
    pltpu.make_async_copy(laid, cloud, out_sem).wait()


def body(crm_state, gcm_state, mass, dest, cost_class):
    any_space = pl.BlockSpec(memory_space=pl.ANY)
    gcm_rows = gcm_state.transpose(0, 2, 3, 4, 5, 1).reshape(FIELDS, OWNED, LEVELS)
    mass_rows = mass.transpose(1, 2, 3, 4, 0).reshape(OWNED, LEVELS)
    landed, gcm_out = pl.pallas_call(
        cloud_kernel,
        out_shape=(
            jax.ShapeDtypeStruct((BLOCKS, BLOCK_ROWS, 128), jnp.float32),
            jax.ShapeDtypeStruct((FIELDS, OWNED, LEVELS), jnp.float32),
        ),
        in_specs=[pl.BlockSpec(memory_space=pltpu.HBM)] * 5,
        out_specs=(any_space, any_space),
        scratch_shapes=[
            pltpu.VMEM((FIELDS, LEVELS + 2, 48, OWNED), jnp.float32),
            pltpu.VMEM((FIELDS, LEVELS + 2, 48, OWNED), jnp.float32),
            pltpu.VMEM((FIELDS, LEVELS, WIDTH, OWNED), jnp.float32),
            pltpu.VMEM((FIELDS * LEVELS, OWNED), jnp.float32),
            pltpu.VMEM((FIELDS * LEVELS, OWNED), jnp.float32),
            pltpu.VMEM((128, OWNED), jnp.float32),
            pltpu.VMEM((HALO_ROWS, 128), jnp.float32),
            pltpu.VMEM((HALO_ROWS, 128), jnp.float32),
            pltpu.VMEM((BLOCKS, BLOCK_ROWS, 128), jnp.float32),
            pltpu.VMEM((FIELDS, OWNED, LEVELS), jnp.float32),
            pltpu.VMEM((FIELDS, OWNED, LEVELS), jnp.float32),
            pltpu.VMEM((OWNED, LEVELS), jnp.float32),
            pltpu.VMEM((1, OWNED), jnp.int32),
            pltpu.VMEM((1, OWNED), jnp.int32),
            pltpu.SemaphoreType.DMA((6,)),
            pltpu.SemaphoreType.REGULAR((2,)),
            pltpu.SemaphoreType.DMA,
            pltpu.SemaphoreType.DMA,
            pltpu.SemaphoreType.DMA,
            pltpu.SemaphoreType.DMA,
            pltpu.SemaphoreType.DMA,
        ],
        compiler_params=pltpu.CompilerParams(
            collective_id=0, has_side_effects=True, vmem_limit_bytes=40 * 2**20
        ),
        name="clouds",
    )(*(pltpu.with_memory_space_constraint(v, pltpu.HBM) for v in (crm_state, gcm_rows, mass_rows, dest.reshape(1, OWNED), cost_class.reshape(1, OWNED))))
    cloud, gcm_out = pl.pallas_call(
        unpack_kernel,
        out_shape=(
            jax.ShapeDtypeStruct((FIELDS, LEVELS * WIDTH, 2 * DEVICES), jnp.float32),
            jax.ShapeDtypeStruct((FIELDS, OWNED, LEVELS), jnp.float32),
        ),
        in_specs=[pl.BlockSpec(memory_space=pltpu.VMEM), pl.BlockSpec(memory_space=pltpu.VMEM)],
        out_specs=(any_space, any_space),
        scratch_shapes=[
            pltpu.VMEM((FIELDS, LEVELS * WIDTH, 2 * DEVICES), jnp.float32),
            pltpu.SemaphoreType.DMA,
            pltpu.SemaphoreType.DMA,
        ],
        compiler_params=pltpu.CompilerParams(vmem_limit_bytes=16 * 2**20),
        name="unpack",
    )(landed, gcm_out)
    cloud = cloud.reshape(FIELDS, LEVELS, WIDTH, 2 * DEVICES)
    gcm_out = gcm_out.reshape(FIELDS, 4, 2, 4, 4, LEVELS).transpose(0, 5, 1, 2, 3, 4)
    return cloud, gcm_out


def solution(mesh):
    return jax.shard_map(
        body,
        mesh=mesh,
        in_specs=(
            P(None, None, None, ("ex", "ey")),
            P(None, None, "ex", "ey", None, None),
            P(None, "ex", "ey", None, None),
            P(("ex", "ey"), None),
            P(("ex", "ey")),
        ),
        out_specs=(P(None, None, None, ("ex", "ey")), P(None, None, "ex", "ey", None, None)),
        check_vma=False,
    )
```
